512 devices in a mesh: group: 8 (over z), dom: 64 (over y, x, core).
Axes of the slice: x: 4, y: 8, z: 8, core: 2. Of those that a mesh axis runs over, the one named last changes fastest.
Arguments:
- orbitals: bfloat16 [1572864, 512], P(('group', 'dom')), may hold values from -6 to 6
- density_rows: bfloat16 [16384, 2048], P(('group', 'dom')), may hold values from -0.01171875 to 0.01171875
- near_blocks: int32 [512, 32], P(('group', 'dom')), may hold values from 0 to 127, as said below
- leaf_coords: int32 [3, 3072], P(None, ('group', 'dom')), may hold values from 0 to 127, as said below
- near_leaves: int32 [3072, 3], P(('group', 'dom')), may hold values from 0 to 17, as said below
- leaf_basis: float32 [64, 1572864], P(None, ('group', 'dom')), may hold values from -2 to 2
- leaf_transfer: float32 [3072, 64, 64], P(('group', 'dom')), may hold values from -0.75 to 0.75
- dev_transfer: float32 [512, 64, 64], P(('group', 'dom')), may hold values from -0.375 to 0.375
- dev_far: int32 [512, 64], P(('group', 'dom')), may hold values 0 or 1
- group_far: int32 [8, 8], P('group'), may hold values 0 or 1
Outputs:
- density: float32 [1572864], P(('group', 'dom'))
- hartree: float32 [1572864], P(('group', 'dom'))
The draws below stay inside these ranges and needn't reach their ends.
Inputs may be any that keep to these rules, and one draw needn't show every extreme that they name: `near_blocks`: each row names 32 distinct blocks of its own coarse domain; block b is rows b * 16 to b * 16 + 15 of the domain's density matrix, held by the device of dom index b // 2. The first 2 entries of every row of a domain are the same: all blocks of one device of that domain, in order. Every other entry is a block held by a device whose dom index differs from the row's own by at most 8, counted cyclically over the 64 dom indices. `near_leaves`: each row names 3 distinct window positions, among them the leaf's own position 6 + (t mod 6) for row t. `leaf_coords`: distinct positions for all leaves.
All inputs are finite; a program needn't handle non-finite values. No bound on the sum of `dev_far` or of `group_far` on one device may be relied on, other than what follows from the above.
Results may differ from the reference program's by a relative error of at most 0.0003.
Values may be sent and summed in bfloat16 or wider, within the bound.
A program may use at most 128 MiB of HBM per device.

```python
import math
import jax
import jax.numpy as jnp
from jax import lax

SIDE = 8
LEAF = 512
CHEB = 4
R = 64
BW = 16
NEAR_B = 32
BLK_DEV = 2
REACH = 8
LEAVES_DEV = 6
NEARL = 3
BLOCKS_G = 128
DEV_COUNT = 512
GRID = 1572864
N_GROUP = 8
N_DOM = 64


def draw_near_blocks(key, part):
    hot_key, noise_key = jax.random.split(jax.random.fold_in(key, 11))
    dev_total_count = N_GROUP * N_DOM
    candidates = N_DOM * BLK_DEV
    hot_owner = jax.random.randint(hot_key, (N_GROUP,), 0, N_DOM)
    noise = jax.random.randint(noise_key, (dev_total_count, candidates), 0, 1024)
    dev_index = jnp.arange(dev_total_count)
    group_index = dev_index // N_DOM
    dom_index = dev_index % N_DOM
    cand_index = jnp.arange(candidates)
    owner = cand_index // BLK_DEV
    apart = jnp.abs(owner[None, :] - dom_index[:, None])
    cyclic = jnp.minimum(apart, N_DOM - apart)
    score = (noise + 1) * candidates + (candidates - 1 - cand_index)[None, :]
    own_hot = hot_owner[group_index]
    is_hot = owner[None, :] == own_hot[:, None]
    blocked = is_hot | (cyclic > REACH)
    score = jnp.where(blocked, -1 - cand_index[None, :], score)
    picked = lax.top_k(score, NEAR_B - BLK_DEV)[1]
    hot_blocks = own_hot[:, None] * BLK_DEV + jnp.arange(BLK_DEV)[None, :]
    return jnp.concatenate([hot_blocks, picked], axis=1).astype(jnp.int32)


def draw_near_leaves(key, part):
    noise_key = jax.random.fold_in(key, 23)
    row_total = N_GROUP * N_DOM * LEAVES_DEV
    window = 3 * LEAVES_DEV
    noise = jax.random.randint(noise_key, (row_total, window), 0, 1024)
    position = jnp.arange(window)
    score = noise * window + position[None, :]
    own_position = LEAVES_DEV + jnp.arange(row_total) % LEAVES_DEV
    score = jnp.where(position[None, :] == own_position[:, None], 1 << 28, score)
    return lax.top_k(score, NEARL)[1].astype(jnp.int32)


def draw_leaf_coords(key, part):
    jitter_key = jax.random.fold_in(key, 37)
    row_total = N_GROUP * N_DOM * LEAVES_DEV
    jitter = jax.random.randint(jitter_key, (3, row_total), 0, 2)
    leaf_index = jnp.arange(row_total)
    local_leaf = leaf_index % LEAVES_DEV
    dom_index = leaf_index // LEAVES_DEV % N_DOM
    group_index = leaf_index // (LEAVES_DEV * N_DOM)
    layout = jnp.stack([2 * local_leaf, 2 * dom_index, 2 * group_index])
    return (layout + jitter).astype(jnp.int32)


def with_ends(values, stream_key, low, largest):
    longest = values.shape.index(max(values.shape))
    spots = []
    for shift in (0, 1):
        where = [jax.random.randint(jax.random.fold_in(stream_key, axis), (), 0, length) for axis, length in enumerate(values.shape)]
        where[longest] = (where[longest] + shift) % values.shape[longest]
        spots.append(tuple(where))
    return values.at[spots[0]].set(low).at[spots[1]].set(largest)


def block_scale(rng, dims, shards, least, top_value):
    level = 1.0
    for dim, shards_of in shards:
        draws = jax.random.uniform(jax.random.fold_in(jax.random.fold_in(rng, 6), dim), (shards_of,), jnp.float32, least / len(shards), top_value / len(shards))
        level = level * jnp.repeat(jnp.exp(draws), dims[dim] // shards_of).reshape((-1,) + (1,) * (len(dims) - 1 - dim))
    return level


def gaussian(rng, extent, spread, bound, shards=(), held_as=jnp.bfloat16):
    entries = spread * jax.random.normal(rng, extent, jnp.float32)
    if shards:
        entries = entries * block_scale(rng, extent, shards, -0.22, 0.18)
    return jnp.clip(entries, -bound, bound).astype(held_as)


def setup_inputs(seed: int = 0) -> dict:
    streams_of = jax.random.split(jax.random.key(seed), 11)
    orbitals = gaussian(streams_of[0], (GRID, NEAR_B * BW), 1.0, 6.0, ((0, 512),))
    density_rows = gaussian(streams_of[1], (N_GROUP * BLOCKS_G * BW, BLOCKS_G * BW), ((NEAR_B * BW) * (NEAR_B * BW)) ** -0.5, 0.01171875, ((0, 512),))
    near_blocks = draw_near_blocks(jax.random.fold_in(streams_of[10], 71), 0)
    leaf_coords = draw_leaf_coords(jax.random.fold_in(streams_of[10], 71), 0)
    near_leaves = draw_near_leaves(jax.random.fold_in(streams_of[10], 71), 0)
    leaf_basis = gaussian(streams_of[5], (R, GRID), 0.125, 2.0, ((1, 512),), jnp.float32)
    leaf_transfer = gaussian(streams_of[6], (DEV_COUNT * LEAVES_DEV, R, R), R ** -0.5, 0.75, ((0, 512),), jnp.float32)
    dev_transfer = gaussian(streams_of[7], (DEV_COUNT, R, R), (4 * R) ** -0.5, 0.375, ((0, 512),), jnp.float32)
    dev_far = with_ends((jax.random.randint(streams_of[8], (DEV_COUNT, N_DOM), 0, 2) < 1).astype(jnp.int32), jax.random.fold_in(streams_of[8], 1), 0, 1)
    group_far = with_ends((jax.random.randint(streams_of[9], (N_GROUP, N_GROUP), 0, 2) < 1).astype(jnp.int32), jax.random.fold_in(streams_of[9], 1), 0, 1)
    return dict(orbitals=orbitals, density_rows=density_rows, near_blocks=near_blocks, leaf_coords=leaf_coords, near_leaves=near_leaves, leaf_basis=leaf_basis, leaf_transfer=leaf_transfer, dev_transfer=dev_transfer, dev_far=dev_far, group_far=group_far)


vol_weight = 0.1
soft_square = 1.0

def coulomb(target, source):
    diff_x = target[0][:, None] - source[0][None, :]
    diff_y = target[1][:, None] - source[1][None, :]
    diff_z = target[2][:, None] - source[2][None, :]
    return 1.0 / jnp.sqrt(diff_x * diff_x + diff_y * diff_y + diff_z * diff_z + soft_square)

def cluster_nodes(bounds):
    steps_idx = jnp.arange(CHEB).astype(jnp.float32)
    cheb_points = jnp.cos((2.0 * steps_idx + 1.0) * (math.pi / (2.0 * CHEB)))
    centre = 0.5 * (bounds[:3] + bounds[3:])
    half_size = 0.5 * (bounds[3:] - bounds[:3])
    along = centre[:, None] + half_size[:, None] * cheb_points[None, :]
    node_index = jnp.arange(CHEB * CHEB * CHEB)
    first = node_index // (CHEB * CHEB)
    second = node_index // CHEB % CHEB
    third = node_index % CHEB
    return jnp.stack([along[0][first], along[1][second], along[2][third]])

def point_offsets():
    place = jnp.arange(LEAF)
    return jnp.stack([place // (SIDE * SIDE), place // SIDE % SIDE, place % SIDE]).astype(jnp.float32)

def reference(orbitals, density_rows, near_blocks, leaf_coords, near_leaves, leaf_basis, leaf_transfer, dev_transfer, dev_far, group_far):
    dev_total_count = N_GROUP * N_DOM
    leaf_count = LEAVES_DEV
    near_width = NEAR_B * BW
    block_total = BLK_DEV * N_DOM
    rows_all = density_rows.reshape(N_GROUP, block_total, BW, block_total, BW)
    orb_all = orbitals.reshape(dev_total_count, leaf_count * LEAF, near_width)

    def density_one(dev_index):
        group_index = dev_index // N_DOM
        near_list = near_blocks[dev_index]
        table = rows_all[group_index]
        tiles = table[near_list[:, None], :, near_list[None, :], :]
        local_matrix = jnp.transpose(tiles, (0, 2, 1, 3)).reshape(near_width, near_width)
        product = jnp.dot(orb_all[dev_index], local_matrix, preferred_element_type=jnp.float32)
        return lax.optimization_barrier(jnp.sum(product * orb_all[dev_index].astype(jnp.float32), axis=1))
    density = lax.map(density_one, jnp.arange(dev_total_count))
    leaf_total = dev_total_count * leaf_count
    coords_f = leaf_coords.astype(jnp.float32)
    points = SIDE * coords_f.T[:, :, None] + point_offsets()[None]
    rho_leaf = density.reshape(leaf_total, LEAF)
    packed = jnp.concatenate([points, rho_leaf[:, None, :]], axis=1)
    packed = packed.reshape(N_GROUP, N_DOM * leaf_count, 4, LEAF)
    padded = jnp.pad(packed, ((0, 0), (leaf_count, leaf_count), (0, 0), (0, 0)))

    def near_one(leaf_index):
        group_index = leaf_index // (N_DOM * leaf_count)
        within = leaf_index % (N_DOM * leaf_count)
        base = within - within % leaf_count
        own_points = points[leaf_index]
        running = jnp.zeros((LEAF,), jnp.float32)
        for near_slot in range(NEARL):
            source = padded[group_index, base + near_leaves[leaf_index, near_slot]]
            running = running + jnp.dot(coulomb(own_points, source[:3]), source[3], precision=lax.Precision.HIGHEST)
        return running
    near_part = lax.map(near_one, jnp.arange(leaf_total)) * vol_weight
    rank = leaf_basis.shape[0]
    leaf_bases = leaf_basis.reshape(rank, leaf_total, LEAF)
    leaf_mom = jnp.einsum('rtp,tp->tr', leaf_bases, rho_leaf, precision=lax.Precision.HIGHEST)
    transfer_four = leaf_transfer.reshape(dev_total_count, leaf_count, rank, rank)
    dev_mom = jnp.einsum('dlqr,dlq->dr', transfer_four, leaf_mom.reshape(dev_total_count, leaf_count, rank), precision=lax.Precision.HIGHEST)
    coords_dev = coords_f.reshape(3, dev_total_count, leaf_count)
    low_side = SIDE * lax.optimization_barrier(jnp.min(coords_dev, axis=2)).T
    high_side = SIDE * lax.optimization_barrier(jnp.max(coords_dev, axis=2)).T + (SIDE - 1)
    bounds_all = jnp.concatenate([low_side, high_side], axis=1)
    nodes_all = jax.vmap(cluster_nodes)(bounds_all)
    upward = jnp.einsum('dqr,dq->dr', dev_transfer, dev_mom, precision=lax.Precision.HIGHEST)
    group_mom = lax.optimization_barrier(jnp.sum(upward.reshape(N_GROUP, N_DOM, rank), axis=1))
    nodes_grouped = nodes_all.reshape(N_GROUP, N_DOM, 3, rank)
    mom_grouped = dev_mom.reshape(N_GROUP, N_DOM, rank)

    def device_one(dev_index):
        group_index = dev_index // N_DOM
        coupling = jax.vmap(lambda other: coulomb(nodes_all[dev_index], other))(nodes_grouped[group_index])
        coupling = coupling * dev_far[dev_index].astype(jnp.float32)[:, None, None]
        return vol_weight * jnp.einsum('srq,sq->r', coupling, mom_grouped[group_index], precision=lax.Precision.HIGHEST)
    dev_local = lax.map(device_one, jnp.arange(dev_total_count))
    bounds_grouped = bounds_all.reshape(N_GROUP, N_DOM, 6)
    group_bounds = jnp.concatenate([lax.optimization_barrier(jnp.min(bounds_grouped[:, :, :3], axis=1)), lax.optimization_barrier(jnp.max(bounds_grouped[:, :, 3:], axis=1))], axis=1)
    group_nodes = jax.vmap(cluster_nodes)(group_bounds)

    def group_one(group_index):
        coupling = jax.vmap(lambda other: coulomb(group_nodes[group_index], other))(group_nodes)
        coupling = coupling * group_far[group_index].astype(jnp.float32)[:, None, None]
        return vol_weight * jnp.einsum('srq,sq->r', coupling, group_mom, precision=lax.Precision.HIGHEST)
    group_local = lax.map(group_one, jnp.arange(N_GROUP))
    group_each = jnp.repeat(group_local, N_DOM, axis=0)
    dev_total = dev_local + jnp.einsum('dqr,dr->dq', dev_transfer, group_each, precision=lax.Precision.HIGHEST)
    leaf_local = jnp.einsum('dlqr,dr->dlq', transfer_four, dev_total, precision=lax.Precision.HIGHEST)
    far_part = jnp.einsum('rtp,tr->tp', leaf_bases, leaf_local.reshape(leaf_total, rank), precision=lax.Precision.HIGHEST)
    hartree = (near_part + far_part).reshape(-1)
    return (density.reshape(-1), hartree)
```

```python
import functools
import math

import jax
import jax.numpy as jnp
from jax import lax
from jax.experimental import pallas as pl
from jax.experimental.pallas import tpu as pltpu
from jax.sharding import PartitionSpec as P

SIDE = 8
LEAF = 512
CHEB = 4
R = 64
BW = 16
NEAR_B = 32
REACH = 8
LEAVES = 6
NEARL = 3
N_DOM = 64
N_GROUP = 8
ROW = 8
CHUNK = 128
WIDE = 6 * CHUNK

vol_weight = 0.1
MESH = pl.DeviceIdType.MESH
F32 = jnp.float32
BF16 = jnp.bfloat16
CHEB_X = [math.cos((2 * a + 1) * math.pi / (2 * CHEB)) for a in range(CHEB)]


def lanes(start, size):
    return pl.ds(pl.multiple_of(start, size), size)


def remote(src, dst, send, recv, device):
    return pltpu.make_async_remote_copy(
        src_ref=src, dst_ref=dst, send_sem=send, recv_sem=recv, device_id=device, device_id_type=MESH
    )


def signal(barrier, device):
    pl.semaphore_signal(barrier, inc=1, device_id=device, device_id_type=MESH)


def choose(pieces, index):
    piece = pieces[0]
    for s in range(1, ROW):
        piece = jnp.where(index == s, pieces[s], piece)
    return piece


def rows_kernel(
    near, rows, window, hot_rows, stage, first, passed, second, kept,
    w_send, w_recv, h_send, h_recv,
):
    me = lax.axis_index("dom")
    y, j = me // ROW, me % ROW
    barrier = pltpu.get_barrier_semaphore()
    offsets = [s * o for o in range(1, REACH + 1) for s in (1, -1)]
    far_rows = [dy for dy in range(1, ROW) if dy not in (1, ROW - 1)]
    for o in offsets:
        signal(barrier, {"dom": (me + o + N_DOM) % N_DOM})
    for dy in far_rows:
        signal(barrier, {"dom": (me + dy * ROW) % N_DOM})

    hot = near[0, 0] // 2
    base = (me + N_DOM - REACH) // 4
    shared = rows[:, :CHUNK]
    for c in range(1, 16):
        shared = jnp.where(hot // 4 == c, rows[:, c * CHUNK : (c + 1) * CHUNK], shared)
    for kk in range(5):
        for c in range(5):
            chunk = (base + kk + c - 2) % 16
            stage[kk, :, c * CHUNK : (c + 1) * CHUNK] = rows[:, lanes(chunk * CHUNK, CHUNK)]
        stage[kk, :, 5 * CHUNK :] = shared
    window[REACH] = stage[2]
    first[j] = rows[:, lanes(j * 256, 256)]
    pl.semaphore_wait(barrier, len(offsets) + len(far_rows))

    def row_peer(d):
        return {"dom": y * ROW + (j + d) % ROW}

    scatter = []
    for d in range(1, ROW):
        to = (j + d) % ROW
        copy = remote(
            rows.at[:, lanes(to * 256, 256)], first.at[j], h_send.at[0, d], h_recv.at[0, d], row_peer(d)
        )
        copy.start()
        scatter.append(copy)
    wide = []
    for n, o in enumerate(offsets):
        kk = (me + o + N_DOM) // 4 - base
        copy = remote(
            stage.at[kk],
            window.at[REACH - o],
            w_send.at[n],
            w_recv.at[n],
            {"dom": (me + o + N_DOM) % N_DOM},
        )
        copy.start()
        wide.append(copy)
    for copy in scatter:
        copy.wait_recv()
    piece = choose(first, hot % ROW)
    passed[...] = piece
    second[y] = piece
    column = []
    for d in range(1, ROW):
        copy = remote(
            passed, second.at[y], h_send.at[1, d], h_recv.at[1, d], {"dom": (me + d * ROW) % N_DOM}
        )
        copy.start()
        column.append(copy)
    for copy in column:
        copy.wait_recv()
    piece = choose(second, hot // ROW)
    kept[...] = piece
    hot_rows[j] = piece
    gather = []
    for d in range(1, ROW):
        copy = remote(kept, hot_rows.at[j], h_send.at[2, d], h_recv.at[2, d], row_peer(d))
        copy.start()
        gather.append(copy)
    for copy in gather + wide:
        copy.wait_recv()
    for copy in scatter + column + gather + wide:
        copy.wait_send()


def exchange_rows(near_blocks, density_rows):
    return pl.pallas_call(
        rows_kernel,
        out_shape=(
            jax.ShapeDtypeStruct((2 * REACH + 1, 32, WIDE), BF16),
            jax.ShapeDtypeStruct((ROW, 32, 256), BF16),
        ),
        in_specs=[
            pl.BlockSpec(memory_space=pltpu.SMEM),
            pl.BlockSpec(memory_space=pltpu.VMEM),
        ],
        out_specs=(
            pl.BlockSpec(memory_space=pltpu.VMEM),
            pl.BlockSpec(memory_space=pltpu.VMEM),
        ),
        scratch_shapes=[
            pltpu.VMEM((5, 32, WIDE), BF16),
            pltpu.VMEM((ROW, 32, 256), BF16),
            pltpu.VMEM((32, 256), BF16),
            pltpu.VMEM((ROW, 32, 256), BF16),
            pltpu.VMEM((32, 256), BF16),
            pltpu.SemaphoreType.DMA((2 * REACH,)),
            pltpu.SemaphoreType.DMA((2 * REACH,)),
            pltpu.SemaphoreType.DMA((3, ROW)),
            pltpu.SemaphoreType.DMA((3, ROW)),
        ],
        compiler_params=pltpu.CompilerParams(collective_id=0, has_side_effects=True),
    )(near_blocks, density_rows)


def eye64():
    return lax.broadcasted_iota(jnp.int32, (R, R), 0) == lax.broadcasted_iota(jnp.int32, (R, R), 1)


def to_column(row):
    return jnp.sum(jnp.where(eye64(), row, 0.0), axis=1, keepdims=True)


def to_row(column):
    return jnp.sum(jnp.where(eye64(), column, 0.0), axis=0, keepdims=True)


def density_kernel(
    near, coords, place, window, hot_rows, orbitals, basis, transfer, dev_transfer,
    rho_out, message, chosen, local_matrix, moments,
):
    leaf = pl.program_id(0)

    @pl.when(leaf == 0)
    def _():
        me = place[0]
        for k in range(2):
            part = slice(k * BW, (k + 1) * BW)
            for c in range(6):
                chunk = (me // 4 + 14 + c) % 16 if c < 5 else near[0, 0] // 8
                chosen[part, c * CHUNK : (c + 1) * CHUNK] = hot_rows[
                    chunk // 2, part, lanes(chunk % 2 * CHUNK, CHUNK)
                ]
        for k in range(2, NEAR_B):
            block = near[0, k]
            slot = (block // 2 - me + REACH + N_DOM) % N_DOM
            chosen[k * BW : (k + 1) * BW, :] = window[slot, lanes(block % 2 * BW, BW), :]
        lane = lax.broadcasted_iota(jnp.int32, (1, LEAF), 1)
        start = jnp.zeros((1, LEAF), jnp.int32)
        for k in range(NEAR_B):
            block = near[0, k]
            chunk = 5 if k < 2 else (block // 8 - me // 4 + 18) % 16
            start = jnp.where(lane // BW == k, chunk * CHUNK + block % 8 * BW, start)
        start = start + lane % BW
        select = lax.broadcasted_iota(jnp.int32, (WIDE, LEAF), 0) == start
        select = jnp.where(select, 1.0, 0.0).astype(BF16)
        local_matrix[...] = jnp.dot(chosen[...], select, preferred_element_type=F32).astype(BF16)
        moments[...] = jnp.zeros_like(moments)

    values = orbitals[...]
    product = jnp.dot(values, local_matrix[...], preferred_element_type=F32)
    product = product * values.astype(F32)
    folded = (product[:, :128] + product[:, 128:256]) + (product[:, 256:384] + product[:, 384:])
    rho = jnp.sum(folded.T, axis=0, keepdims=True)
    for i in range(4):
        rho_out[pl.ds(leaf * 4 + i, 1), :] = rho[:, i * 128 : (i + 1) * 128]
    leaf_moments = jnp.sum(basis[...] * rho, axis=1, keepdims=True)
    moments[...] += jnp.sum(transfer[0] * leaf_moments, axis=0, keepdims=True)

    @pl.when(leaf == LEAVES - 1)
    def _():
        mine = moments[...]
        upward = jnp.sum(dev_transfer[0] * to_column(mine), axis=0, keepdims=True)
        message[0:1, :] = jnp.concatenate([mine, upward], axis=1)
        lane = lax.broadcasted_iota(jnp.int32, (1, 128), 1)
        packed = jnp.zeros((1, 128), jnp.int32)
        for d in range(3):
            low = high = coords[d, 0]
            for t in range(1, LEAVES):
                low = jnp.minimum(low, coords[d, t])
                high = jnp.maximum(high, coords[d, t])
            packed = jnp.where(lane == d, low, packed)
            packed = jnp.where(lane == 3 + d, high, packed)
            for t in range(LEAVES):
                packed = jnp.where(lane == 8 + 3 * t + d, coords[d, t], packed)
        message[1:2, :] = packed.astype(F32)


def density_and_moments(
    near_blocks, leaf_coords, place, window, hot_rows, orbitals, basis, leaf_transfer, dev_transfer
):
    whole = lambda shape: pl.BlockSpec(shape, lambda t: (0,) * len(shape))
    return pl.pallas_call(
        density_kernel,
        grid=(LEAVES,),
        out_shape=(
            jax.ShapeDtypeStruct((4 * LEAVES, 128), F32),
            jax.ShapeDtypeStruct((2, 128), F32),
        ),
        in_specs=[
            pl.BlockSpec(memory_space=pltpu.SMEM),
            pl.BlockSpec(memory_space=pltpu.SMEM),
            pl.BlockSpec(memory_space=pltpu.SMEM),
            whole((2 * REACH + 1, 32, WIDE)),
            whole((ROW, 32, 256)),
            pl.BlockSpec((LEAF, LEAF), lambda t: (t, 0)),
            pl.BlockSpec((R, LEAF), lambda t: (0, t)),
            pl.BlockSpec((1, R, R), lambda t: (t, 0, 0)),
            whole((1, R, R)),
        ],
        out_specs=(whole((4 * LEAVES, 128)), whole((2, 128))),
        scratch_shapes=[
            pltpu.VMEM((LEAF, WIDE), BF16),
            pltpu.VMEM((LEAF, LEAF), BF16),
            pltpu.VMEM((1, R), F32),
        ],
        compiler_params=pltpu.CompilerParams(vmem_limit_bytes=32 << 20),
    )(near_blocks, leaf_coords, place, window, hot_rows, orbitals, basis, leaf_transfer, dev_transfer)


def moments_kernel(
    rho, message, halo, everyone, domains, mine, total, halo_send, halo_recv, m_send, m_recv
):
    me = lax.axis_index("dom")
    group = lax.axis_index("group")
    y, j = me // ROW, me % ROW
    barrier = pltpu.get_barrier_semaphore()
    before, after = {"dom": (me + N_DOM - 1) % N_DOM}, {"dom": (me + 1) % N_DOM}
    row_peers = [{"dom": y * ROW + (j + d) % ROW} for d in range(1, ROW)]
    column_peers = [{"dom": (me + d * ROW) % N_DOM} for d in range(1, ROW)]
    group_peers = [{"group": (group + d) % N_GROUP} for d in range(1, N_GROUP)]
    peers = row_peers + column_peers + group_peers + [before, after]
    for peer in peers:
        signal(barrier, peer)
    mine[j] = message[...]
    pl.semaphore_wait(barrier, len(peers))

    def send_all(phase, src, dst, targets):
        copies = []
        for d, peer in enumerate(targets):
            copy = remote(src, dst, m_send.at[phase, d], m_recv.at[phase, d], peer)
            copy.start()
            copies.append(copy)
        return copies

    first = send_all(0, message, mine.at[j], row_peers)
    up = remote(rho, halo.at[0], halo_send.at[0], halo_recv.at[0], after)
    up.start()
    down = remote(rho, halo.at[1], halo_send.at[1], halo_recv.at[1], before)
    down.start()
    for copy in first:
        copy.wait_recv()
    everyone[y] = mine[...]
    second = send_all(1, mine, everyone.at[y], column_peers)
    for copy in second:
        copy.wait_recv()
    lane = lax.broadcasted_iota(jnp.int32, (2, 128), 1)
    sums, low, high = (jnp.zeros((2, 128), F32), everyone[0, 0], everyone[0, 0])
    for a in range(ROW):
        for b in range(ROW):
            value = everyone[a, b]
            sums, low, high = (sums + value, jnp.minimum(low, value), jnp.maximum(high, value))
    sums = pltpu.roll(sums, 64, 1)
    is_first = lax.broadcasted_iota(jnp.int32, (2, 128), 0) == 0
    packed = jnp.where(is_first, sums, jnp.where(lane < 3, low, high))
    total[...] = packed
    domains[group] = packed
    third = send_all(2, total, domains.at[group], group_peers)
    for copy in third + [up, down]:
        copy.wait_recv()
    for copy in first + second + third + [up, down]:
        copy.wait_send()


def exchange_moments(rho, message):
    vmem = pl.BlockSpec(memory_space=pltpu.VMEM)
    return pl.pallas_call(
        moments_kernel,
        out_shape=(
            jax.ShapeDtypeStruct((2, 4 * LEAVES, 128), F32),
            jax.ShapeDtypeStruct((ROW, ROW, 2, 128), F32),
            jax.ShapeDtypeStruct((N_GROUP, 2, 128), F32),
        ),
        in_specs=[vmem, vmem],
        out_specs=(vmem, vmem, vmem),
        scratch_shapes=[
            pltpu.VMEM((ROW, 2, 128), F32),
            pltpu.VMEM((2, 128), F32),
            pltpu.SemaphoreType.DMA((2,)),
            pltpu.SemaphoreType.DMA((2,)),
            pltpu.SemaphoreType.DMA((3, ROW)),
            pltpu.SemaphoreType.DMA((3, ROW)),
        ],
        compiler_params=pltpu.CompilerParams(collective_id=1, has_side_effects=True),
    )(rho, message)


def split(value):
    high = value.astype(BF16)
    return high, (value - high.astype(F32)).astype(BF16)


def potential_kernel(
    coords, near_leaves, place, rho, halo, everyone, domains, dev_far, group_far, dev_transfer,
    leaf_transfer, basis, out, rho_rows, sources, spots, table, rows_of, bounds_of, partial,
):
    me = place[0]
    rows_of[...] = jnp.zeros_like(rows_of)
    bounds_of[...] = jnp.zeros_like(bounds_of)
    rows_of[0:N_DOM, :] = everyone[pl.ds(0, N_DOM, stride=2), :]
    bounds_of[0:N_DOM, :] = everyone[pl.ds(1, N_DOM, stride=2), :]
    rows_of[N_DOM : N_DOM + N_GROUP, :] = domains[pl.ds(0, N_GROUP, stride=2), :]
    bounds_of[N_DOM : N_DOM + N_GROUP, :] = domains[pl.ds(1, N_GROUP, stride=2), :]
    mask = jnp.concatenate(
        [dev_far[...], group_far[...], jnp.zeros((1, 128 - N_DOM - N_GROUP), jnp.int32)], axis=1
    ).astype(F32)
    weights = rows_of[...].T[:R, :] * mask
    edges = bounds_of[...].T[:8, :]
    lane = lax.broadcasted_iota(jnp.int32, (1, 128), 1)
    is_dev = lane < N_DOM
    own, other = [], []
    sub = lax.broadcasted_iota(jnp.int32, (8, 128), 0)
    for d in range(3):
        low, high = SIDE * edges[d : d + 1], SIDE * edges[3 + d : 4 + d] + (SIDE - 1)
        first = last = coords[d, 0]
        for t in range(1, LEAVES):
            first = jnp.minimum(first, coords[d, t])
            last = jnp.maximum(last, coords[d, t])
        all_low = jnp.min(jnp.where(is_dev, low, 1e9), axis=1, keepdims=True)
        all_high = jnp.max(jnp.where(is_dev, high, -1e9), axis=1, keepdims=True)
        own_low = jnp.where(is_dev, (SIDE * first).astype(F32), all_low)
        own_high = jnp.where(is_dev, (SIDE * last + (SIDE - 1)).astype(F32), all_high)
        own.append((0.5 * (own_low + own_high), 0.5 * (own_high - own_low)))
        other.append((0.5 * (low + high), 0.5 * (high - low)))

    def pick(index):
        value = jnp.full((8, 128), CHEB_X[0], F32)
        for a in range(1, CHEB):
            value = jnp.where(index == a, CHEB_X[a], value)
        return value

    sites = [[c + h * x for x in CHEB_X] for c, h in own]
    xs = [other[0][0] + other[0][1] * x for x in CHEB_X]
    ys = [other[1][0] + other[1][1] * pick(2 * half + sub // 4) for half in range(2)]
    zs = other[2][0] + other[2][1] * pick(sub % 4)
    dx = [[(s - x) * (s - x) for x in xs] for s in sites[0]]
    dy = [[(s - v) * (s - v) for v in ys] for s in sites[1]]
    dz = [(s - zs) * (s - zs) + 1.0 for s in sites[2]]
    for b in range(CHEB):
        for e in range(CHEB):
            tail = [v + dz[e] for v in dy[b]]
            for a in range(CHEB):
                running = jnp.zeros((8, 128), F32)
                for t in range(8):
                    value = lax.rsqrt(dx[a][t // 2] + tail[t % 2])
                    running = running + value * weights[8 * t : 8 * t + 8]
                r = a * 16 + b * 4 + e
                partial[8 * r : 8 * r + 8, :] = running
    summed = partial[pl.ds(0, R, stride=8), :]
    for k in range(1, 8):
        summed = summed + partial[pl.ds(k, R, stride=8), :]
    summed = summed * vol_weight
    dev_local = jnp.sum(jnp.where(is_dev, summed, 0.0), axis=1, keepdims=True)
    group_local = to_row(jnp.sum(jnp.where(is_dev, 0.0, summed), axis=1, keepdims=True))
    dev_total = to_row(dev_local + jnp.sum(dev_transfer[0] * group_local, axis=1, keepdims=True))

    inside = [jnp.where(me > 0, 1.0, 0.0), 1.0, jnp.where(me < N_DOM - 1, 1.0, 0.0)]
    around = [(me + N_DOM - 1) % N_DOM, me, (me + 1) % N_DOM]
    for s, piece in enumerate((halo[0], rho[...], halo[1])):
        piece = piece * inside[s]
        rho_rows[pl.ds(48 * s, 24, stride=2), :] = piece[:, :64]
        rho_rows[pl.ds(48 * s + 1, 24, stride=2), :] = piece[:, 64:]
        held = everyone[pl.ds(2 * around[s] + 1, 1), :]
        for t in range(LEAVES):
            for d in range(3):
                k = 8 + 3 * t + d
                spots[s * LEAVES + t, d : d + 1, :] = jnp.broadcast_to(held[:, k : k + 1], (1, 128))
    for w in range(3 * LEAVES):
        high, low = split(rho_rows[8 * w : 8 * w + 8, :])
        sources[w] = jnp.concatenate(
            [jnp.concatenate([high, high], axis=1), jnp.concatenate([low, low], axis=1)], axis=0
        )
    q = lax.broadcasted_iota(jnp.int32, (64, 128), 0)
    p = lax.broadcasted_iota(jnp.int32, (64, 128), 1) % 64
    gap_y = (p // 8 - q // 8).astype(F32)
    gap_z = (p % 8 - q % 8).astype(F32)
    step = (2 * sub + lax.broadcasted_iota(jnp.int32, (8, 128), 1) // 64 - 7).astype(F32)

    def one_leaf(t, carry):
        here = spots[LEAVES + t]
        lhs = []
        for n in range(NEARL):
            w = near_leaves[t, n]
            shift = SIDE * (here - spots[w])
            x = step + shift[0:1, :]
            yy, zz = gap_y + shift[1:2, :], gap_z + shift[2:3, :]
            x, flat = x * x, yy * yy + zz * zz + 1.0
            for i in range(8):
                high, low = split(lax.rsqrt(flat + x[i : i + 1, :]))
                table[128 * n : 128 * n + 64, 128 * i : 128 * i + 128] = high
                table[128 * n + 64 : 128 * n + 128, 128 * i : 128 * i + 128] = low
            lhs.append(sources[w])
        both = jnp.dot(jnp.concatenate(lhs, axis=1), table[...], preferred_element_type=F32)
        both = both[:8] + both[8:]
        near = jnp.zeros((1, LEAF), F32)
        for qx in range(SIDE):
            near = near + both[qx : qx + 1, (7 - qx) * 64 : (7 - qx) * 64 + LEAF]
        leaf_local = jnp.sum(leaf_transfer[t] * dev_total, axis=1, keepdims=True)
        far = jnp.sum(basis[:, lanes(t * LEAF, LEAF)] * leaf_local, axis=0, keepdims=True)
        value = near * vol_weight + far
        for i in range(4):
            out[pl.ds(4 * t + i, 1), :] = value[:, 128 * i : 128 * i + 128]
        return carry

    lax.fori_loop(0, LEAVES, one_leaf, 0)


def potential(
    leaf_coords, near_leaves, place, rho, halo, everyone, domains, dev_far, group_far, dev_transfer,
    leaf_transfer, basis,
):
    smem, vmem = pl.BlockSpec(memory_space=pltpu.SMEM), pl.BlockSpec(memory_space=pltpu.VMEM)
    return pl.pallas_call(
        potential_kernel,
        out_shape=jax.ShapeDtypeStruct((4 * LEAVES, 128), F32),
        in_specs=[smem] * 3 + [vmem] * 9,
        out_specs=vmem,
        scratch_shapes=[
            pltpu.VMEM((24 * LEAVES, 64), F32),
            pltpu.VMEM((3 * LEAVES, 16, 128), BF16),
            pltpu.VMEM((3 * LEAVES, 8, 128), F32),
            pltpu.VMEM((128 * NEARL, 1024), BF16),
            pltpu.VMEM((128, 128), F32),
            pltpu.VMEM((128, 128), F32),
            pltpu.VMEM((8 * R, 128), F32),
        ],
        compiler_params=pltpu.CompilerParams(vmem_limit_bytes=32 << 20),
    )(
        leaf_coords, near_leaves, place, rho, halo, everyone, domains, dev_far, group_far,
        dev_transfer, leaf_transfer, basis,
    )


def local(
    orbitals, density_rows, near_blocks, leaf_coords, near_leaves, leaf_basis, leaf_transfer,
    dev_transfer, dev_far, group_far,
):
    place = lax.axis_index("dom").astype(jnp.int32)[None]
    window, hot_rows = exchange_rows(near_blocks, density_rows)
    rho, message = density_and_moments(
        near_blocks, leaf_coords, place, window, hot_rows, orbitals, leaf_basis, leaf_transfer,
        dev_transfer,
    )
    halo, everyone, domains = exchange_moments(rho, message)
    hartree = potential(
        leaf_coords, near_leaves, place, rho, halo, everyone.reshape(2 * N_DOM, 128),
        domains.reshape(2 * N_GROUP, 128), dev_far, group_far, dev_transfer, leaf_transfer,
        leaf_basis,
    )
    return (rho.reshape(-1), hartree.reshape(-1))


def solution(mesh):
    in_specs = (
        P(("group", "dom"), None),
        P(("group", "dom"), None),
        P(("group", "dom"), None),
        P(None, ("group", "dom")),
        P(("group", "dom"), None),
        P(None, ("group", "dom")),
        P(("group", "dom"), None, None),
        P(("group", "dom"), None, None),
        P(("group", "dom"), None),
        P("group", None),
    )
    out_specs = (P(("group", "dom")), P(("group", "dom")))
    return jax.shard_map(local, mesh=mesh, in_specs=in_specs, out_specs=out_specs, check_vma=False)
```

```python
import functools
import math

import jax
import jax.numpy as jnp
from jax import lax
from jax.experimental import pallas as pl
from jax.experimental.pallas import tpu as pltpu
from jax.sharding import PartitionSpec as P

SIDE = 8
LEAF = 512
CHEB = 4
R = 64
BW = 16
NEAR_B = 32
REACH = 8
LEAVES = 6
NEARL = 3
N_DOM = 64
N_GROUP = 8
ROW = 8
CHUNK = 128
HELD = 2 * REACH + 1
WIDE = 6 * CHUNK

vol_weight = 0.1
MESH = pl.DeviceIdType.MESH
F32 = jnp.float32
BF16 = jnp.bfloat16
CHEB_X = [math.cos((2 * a + 1) * math.pi / (2 * CHEB)) for a in range(CHEB)]


def lanes(start, size):
    return pl.ds(pl.multiple_of(start, size), size)


def remote(src, dst, send, recv, device):
    return pltpu.make_async_remote_copy(
        src_ref=src, dst_ref=dst, send_sem=send, recv_sem=recv, device_id=device, device_id_type=MESH
    )


def signal(barrier, device):
    pl.semaphore_signal(barrier, inc=1, device_id=device, device_id_type=MESH)


def choose(pieces, index):
    piece = pieces[0]
    for s in range(1, len(pieces)):
        piece = jnp.where(index == s, pieces[s], piece)
    return piece


def eye64():
    return lax.broadcasted_iota(jnp.int32, (R, R), 0) == lax.broadcasted_iota(jnp.int32, (R, R), 1)


def to_column(row):
    return jnp.sum(jnp.where(eye64(), row, 0.0), axis=1, keepdims=True)


def to_row(column):
    return jnp.sum(jnp.where(eye64(), column, 0.0), axis=0, keepdims=True)


def split(value):
    high = value.astype(BF16)
    return high, (value - high.astype(F32)).astype(BF16)


def iota(shape, dim):
    return lax.broadcasted_iota(jnp.int32, shape, dim)


def first_and_last(coords, d):
    first = last = coords[d, 0]
    for t in range(1, LEAVES):
        first = jnp.minimum(first, coords[d, t])
        last = jnp.maximum(last, coords[d, t])
    return first, last


def spread(index, shape):
    value = jnp.full(shape, CHEB_X[0], F32)
    for a in range(1, CHEB):
        value = jnp.where(index == a, CHEB_X[a], value)
    return value


def kernel(
    near, coords, near_leaves,
    orbitals_h, rows_h, basis_h, transfer_h, dev_transfer_h, dev_far, group_far,
    rho, out,
    orbitals, rows, basis, transfer, dev_transfer,
    stage, window, first, passed, second, kept, hot_rows,
    meta_row, meta_all, meta_total, meta_groups,
    mom_mine, mom_row, mom_all, mom_total, mom_groups,
    halo, pick_rows, pick_columns, chosen, local_matrix,
    rho_rows, sources, spots, tables, far_rows, far_bounds, couplings, partial,
    load_sem, w_send, w_recv, h_send, h_recv, m_send, m_recv, u_send, u_recv, e_send, e_recv,
):
    me = lax.axis_index("dom")
    group = lax.axis_index("group")
    y, j = me // ROW, me % ROW
    offsets = [s * o for o in range(REACH, 0, -1) for s in (1, -1)]
    far_columns = [dy for dy in range(2, ROW - 1)]
    row_peers = [{"dom": y * ROW + (j + d) % ROW} for d in range(1, ROW)]
    column_peers = [{"dom": (me + d * ROW) % N_DOM} for d in range(1, ROW)]
    group_peers = [{"group": (group + d) % N_GROUP} for d in range(1, N_GROUP)]
    peers = [{"dom": (me + o + N_DOM) % N_DOM} for o in offsets]
    peers = peers + [column_peers[dy - 1] for dy in far_columns] + group_peers
    barrier = pltpu.get_barrier_semaphore()
    for peer in peers:
        signal(barrier, peer)
    loads = []
    for n, (src, dst) in enumerate(
        (
            (rows_h, rows),
            (orbitals_h, orbitals),
            (basis_h, basis),
            (transfer_h, transfer),
            (dev_transfer_h, dev_transfer),
        )
    ):
        copy = pltpu.make_async_copy(src, dst, load_sem.at[n])
        copy.start()
        loads.append(copy)

    def send_all(src, dst, sends, recvs, phase, targets):
        copies = []
        for d, peer in enumerate(targets):
            copy = remote(src, dst, sends.at[phase, d], recvs.at[phase, d], peer)
            copy.start()
            copies.append(copy)
        return copies

    def arrived(copies):
        for copy in copies:
            copy.wait_recv()

    lane = iota((1, 128), 1)
    packed = jnp.zeros((1, 128), jnp.int32)
    for d in range(3):
        low, high = first_and_last(coords, d)
        packed = jnp.where(lane == d, low, packed)
        packed = jnp.where(lane == 3 + d, high, packed)
        for t in range(LEAVES):
            packed = jnp.where(lane == 8 + 3 * t + d, coords[d, t], packed)
    meta_row[j] = packed.astype(F32)

    loads[0].wait()
    hot = near[0, 0] // 2
    base = (me + N_DOM - REACH) // 4
    shared = choose([rows[:, c * CHUNK : (c + 1) * CHUNK] for c in range(16)], hot // 4)
    for kk in range(5):
        for c in range(5):
            chunk = (base + kk + c - 2) % 16
            stage[kk, :, c * CHUNK : (c + 1) * CHUNK] = rows[:, lanes(chunk * CHUNK, CHUNK)]
        stage[kk, :, 5 * CHUNK :] = shared
    window[REACH] = stage[2]
    first[j] = rows[:, lanes(j * 256, 256)]
    pl.semaphore_wait(barrier, len(peers))

    hot_a = []
    for d in range(1, ROW):
        to = (j + d) % ROW
        copy = remote(
            rows.at[:, lanes(to * 256, 256)], first.at[j], h_send.at[0, d - 1], h_recv.at[0, d - 1],
            row_peers[d - 1],
        )
        copy.start()
        hot_a.append(copy)
    meta_a = send_all(meta_row.at[j], meta_row.at[j], m_send, m_recv, 0, row_peers)
    wide = []
    for n, o in enumerate(offsets):
        kk = (me + o + N_DOM) // 4 - base
        copy = remote(stage.at[kk], window.at[REACH - o], w_send.at[n], w_recv.at[n], peers[n])
        copy.start()
        wide.append(copy)

    gap = iota((BW, 640), 1) - iota((BW, 640), 0)
    for k in range(2, NEAR_B):
        block = near[0, k]
        start = (block // 2 - me + REACH + N_DOM) % N_DOM * 32 + block % 2 * BW
        part = jnp.where(gap == start, 1.0, 0.0)[:, : 32 * HELD]
        pick_rows[(k - 2) * BW : (k - 1) * BW, :] = part.astype(BF16)
    wide_lane = iota((1, LEAF), 1)
    start = jnp.zeros((1, LEAF), jnp.int32)
    for k in range(NEAR_B):
        block = near[0, k]
        chunk = 5 if k < 2 else (block // 8 - me // 4 + 18) % 16
        start = jnp.where(wide_lane // BW == k, chunk * CHUNK + block % 8 * BW, start)
    start = start + wide_lane % BW
    pick = jnp.where(iota((WIDE, LEAF), 0) == start, 1.0, 0.0)
    pick_columns[...] = pick.astype(BF16)

    arrived(hot_a)
    piece = choose([first[s] for s in range(ROW)], hot % ROW)
    passed[...] = piece
    second[y] = piece
    hot_b = send_all(passed, second.at[y], h_send, h_recv, 1, column_peers)
    arrived(meta_a)
    meta_all[y] = meta_row[...]
    meta_b = send_all(meta_row, meta_all.at[y], m_send, m_recv, 1, column_peers)
    arrived(hot_b)
    piece = choose([second[s] for s in range(ROW)], hot // ROW)
    kept[...] = piece
    hot_rows[j] = piece
    hot_c = send_all(kept, hot_rows.at[j], h_send, h_recv, 2, row_peers)
    arrived(meta_b)
    low = high = meta_all[0, 0]
    for a in range(ROW):
        for b in range(ROW):
            value = meta_all[a, b]
            low, high = jnp.minimum(low, value), jnp.maximum(high, value)
    bounds = jnp.where(lane < 3, low, high)
    meta_total[...] = bounds
    meta_groups[group] = bounds
    meta_c = send_all(meta_total, meta_groups.at[group], m_send, m_recv, 2, group_peers)

    around = [(me + N_DOM - 1) % N_DOM, me, (me + 1) % N_DOM]
    for s in range(3):
        held = meta_all[around[s] // ROW, around[s] % ROW]
        for t in range(LEAVES):
            for d in range(3):
                k = 8 + 3 * t + d
                spots[s * LEAVES + t, d : d + 1, :] = jnp.broadcast_to(held[:, k : k + 1], (1, 128))
    q = iota((64, 128), 0)
    p = iota((64, 128), 1) % 64
    gap_y = (p // 8 - q // 8).astype(F32)
    gap_z = (p % 8 - q % 8).astype(F32)
    step = (2 * iota((8, 128), 0) + iota((8, 128), 1) // 64 - 7).astype(F32)

    def build(t, carry):
        here = spots[LEAVES + t]
        for n in range(NEARL):
            w = near_leaves[n, t]
            shift = SIDE * (here - spots[w])
            x = step + shift[0:1, :]
            yy, zz = gap_y + shift[1:2, :], gap_z + shift[2:3, :]
            x, flat = x * x, yy * yy + zz * zz + 1.0
            for i in range(8):
                high, low = split(lax.rsqrt(flat + x[i : i + 1, :]))
                tables[t, 128 * n : 128 * n + 64, 128 * i : 128 * i + 128] = high
                tables[t, 128 * n + 64 : 128 * n + 128, 128 * i : 128 * i + 128] = low
        return carry

    lax.fori_loop(0, LEAVES, build, 0)

    for copy in loads[1:]:
        copy.wait()
    arrived(wide)
    arrived(hot_c)
    for c in range(6):
        part = slice(c * CHUNK, (c + 1) * CHUNK)
        if c < 5:
            chunk = (me // 4 + 14 + c) % 16
            chosen[0:32, part] = hot_rows[chunk // 2, :, lanes(chunk % 2 * CHUNK, CHUNK)]
        else:
            options = [
                hot_rows[a, :, b * CHUNK : (b + 1) * CHUNK] for a in range(ROW) for b in range(2)
            ]
            chosen[0:32, part] = choose(options, hot // 4)
    held = window[...].reshape(32 * HELD, WIDE)
    chosen[32:, :] = jnp.dot(pick_rows[...], held, preferred_element_type=F32).astype(BF16)
    matrix = jnp.dot(chosen[...], pick_columns[...], preferred_element_type=F32)
    local_matrix[...] = matrix.astype(BF16)

    def one_density(t, total):
        values = orbitals[pl.ds(pl.multiple_of(t * LEAF, LEAF), LEAF), :]
        product = jnp.dot(values, local_matrix[...], preferred_element_type=F32)
        product = product * values.astype(F32)
        folded = (product[:, :128] + product[:, 128:256]) + (product[:, 256:384] + product[:, 384:])
        here = jnp.sum(folded.T, axis=0, keepdims=True)
        for i in range(4):
            rho[pl.ds(t * 4 + i, 1), :] = here[:, i * 128 : (i + 1) * 128]
        leaf_moments = jnp.sum(basis[:, lanes(t * LEAF, LEAF)] * here, axis=1, keepdims=True)
        return total + jnp.sum(transfer[t] * leaf_moments, axis=0, keepdims=True)

    mine = lax.fori_loop(0, LEAVES, one_density, jnp.zeros((1, R), F32))
    edge = [
        remote(rho, halo.at[0], e_send.at[0], e_recv.at[0], {"dom": around[2]}),
        remote(rho, halo.at[1], e_send.at[1], e_recv.at[1], {"dom": around[0]}),
    ]
    upward = jnp.sum(dev_transfer[0] * to_column(mine), axis=0, keepdims=True)
    mom_mine[...] = jnp.concatenate([mine, upward], axis=1)
    mom_row[j] = mom_mine[...]
    mom_a = send_all(mom_mine, mom_row.at[j], u_send, u_recv, 0, row_peers)
    for copy in edge:
        copy.start()

    arrived(meta_c)
    far_bounds[...] = jnp.zeros_like(far_bounds)
    for a in range(ROW):
        for b in range(ROW):
            far_bounds[a * ROW + b : a * ROW + b + 1, :] = meta_all[a, b]
        far_bounds[N_DOM + a : N_DOM + a + 1, :] = meta_groups[a]
    edges = far_bounds[...].T[:8, :]
    is_dev = lane < N_DOM
    own, other = [], []
    for d in range(3):
        low, high = SIDE * edges[d : d + 1], SIDE * edges[3 + d : 4 + d] + (SIDE - 1)
        dev_low, dev_high = first_and_last(coords, d)
        all_low, all_high = bounds[:, d : d + 1], bounds[:, 3 + d : 4 + d]
        own_low = SIDE * jnp.where(is_dev, dev_low.astype(F32), all_low)
        own_high = SIDE * jnp.where(is_dev, dev_high.astype(F32), all_high) + (SIDE - 1)
        own.append((0.5 * (own_low + own_high), 0.5 * (own_high - own_low)))
        other.append((0.5 * (low + high), 0.5 * (high - low)))
    sub = iota((8, 128), 0)
    sites = [[c + h * x for x in CHEB_X] for c, h in own]
    xs = [other[0][0] + other[0][1] * x for x in CHEB_X]
    ys = [other[1][0] + other[1][1] * spread(2 * half + sub // 4, (8, 128)) for half in range(2)]
    zs = other[2][0] + other[2][1] * spread(sub % 4, (8, 128))
    dx = [[(s - x) * (s - x) for x in xs] for s in sites[0]]
    dy = [[(s - v) * (s - v) for v in ys] for s in sites[1]]
    dz = [(s - zs) * (s - zs) + 1.0 for s in sites[2]]
    for b in range(CHEB):
        for e in range(CHEB):
            rest = [v + dz[e] for v in dy[b]]
            for a in range(CHEB):
                for t in range(8):
                    r = a * 16 + b * 4 + e
                    couplings[r, 8 * t : 8 * t + 8, :] = lax.rsqrt(dx[a][t // 2] + rest[t % 2])

    arrived(mom_a)
    mom_all[y] = mom_row[...]
    mom_b = send_all(mom_row, mom_all.at[y], u_send, u_recv, 1, column_peers)

    arrived(edge)
    inside = [jnp.where(me > 0, 1.0, 0.0), 1.0, jnp.where(me < N_DOM - 1, 1.0, 0.0)]
    for s, held in enumerate((halo[0], rho[...], halo[1])):
        held = held * inside[s]
        rho_rows[pl.ds(48 * s, 24, stride=2), :] = held[:, :64]
        rho_rows[pl.ds(48 * s + 1, 24, stride=2), :] = held[:, 64:]
    for w in range(3 * LEAVES):
        high, low = split(rho_rows[8 * w : 8 * w + 8, :])
        sources[w] = jnp.concatenate(
            [jnp.concatenate([high, high], axis=1), jnp.concatenate([low, low], axis=1)], axis=0
        )

    def one_near(t, carry):
        lhs = jnp.concatenate([sources[near_leaves[n, t]] for n in range(NEARL)], axis=1)
        both = jnp.dot(lhs, tables[t], preferred_element_type=F32)
        both = both[:8] + both[8:]
        value = jnp.zeros((1, LEAF), F32)
        for qx in range(SIDE):
            value = value + both[qx : qx + 1, (7 - qx) * 64 : (7 - qx) * 64 + LEAF]
        for i in range(4):
            out[pl.ds(4 * t + i, 1), :] = value[:, 128 * i : 128 * i + 128] * vol_weight
        return carry

    arrived(mom_b)
    sums = jnp.zeros((1, 128), F32)
    for a in range(ROW):
        for b in range(ROW):
            sums = sums + mom_all[a, b]
    sums = pltpu.roll(sums, 64, 1)
    mom_total[...] = sums
    mom_groups[group] = sums
    mom_c = send_all(mom_total, mom_groups.at[group], u_send, u_recv, 2, group_peers)
    lax.fori_loop(0, LEAVES, one_near, 0)

    arrived(mom_c)
    far_rows[...] = jnp.zeros_like(far_rows)
    for a in range(ROW):
        for b in range(ROW):
            far_rows[a * ROW + b : a * ROW + b + 1, :] = mom_all[a, b]
        far_rows[N_DOM + a : N_DOM + a + 1, :] = mom_groups[a]
    mask = jnp.concatenate(
        [dev_far[...], group_far[...], jnp.zeros((1, 128 - N_DOM - N_GROUP), jnp.int32)], axis=1
    ).astype(F32)
    weights = far_rows[...].T[:R, :] * mask
    for r in range(R):
        running = jnp.zeros((8, 128), F32)
        for t in range(8):
            part = slice(8 * t, 8 * t + 8)
            running = running + couplings[r, part, :] * weights[part]
        partial[8 * r : 8 * r + 8, :] = running
    summed = partial[pl.ds(0, R, stride=8), :]
    for k in range(1, 8):
        summed = summed + partial[pl.ds(k, R, stride=8), :]
    summed = summed * vol_weight
    dev_local = jnp.sum(jnp.where(is_dev, summed, 0.0), axis=1, keepdims=True)
    group_local = to_row(jnp.sum(jnp.where(is_dev, 0.0, summed), axis=1, keepdims=True))
    dev_total = to_row(dev_local + jnp.sum(dev_transfer[0] * group_local, axis=1, keepdims=True))
    for t in range(LEAVES):
        leaf_local = jnp.sum(transfer[t] * dev_total, axis=1, keepdims=True)
        far = jnp.sum(basis[:, t * LEAF : (t + 1) * LEAF] * leaf_local, axis=0, keepdims=True)
        for i in range(4):
            out[4 * t + i : 4 * t + i + 1, :] += far[:, 128 * i : 128 * i + 128]
    for copy in hot_a + hot_b + hot_c + meta_a + meta_b + meta_c + wide:
        copy.wait_send()
    for copy in mom_a + mom_b + mom_c + edge:
        copy.wait_send()


def local(
    orbitals, density_rows, near_blocks, leaf_coords, near_leaves, leaf_basis, leaf_transfer,
    dev_transfer, dev_far, group_far,
):
    smem, vmem = pl.BlockSpec(memory_space=pltpu.SMEM), pl.BlockSpec(memory_space=pltpu.VMEM)
    anywhere = pl.BlockSpec(memory_space=pl.ANY)
    rows = pltpu.VMEM((1, 128), F32)
    eight = pltpu.VMEM((ROW, 1, 128), F32)
    plane = pltpu.VMEM((ROW, ROW, 1, 128), F32)
    sems = pltpu.SemaphoreType.DMA
    density, hartree = pl.pallas_call(
        kernel,
        out_shape=(
            jax.ShapeDtypeStruct((4 * LEAVES, 128), F32),
            jax.ShapeDtypeStruct((4 * LEAVES, 128), F32),
        ),
        in_specs=[smem] * 3 + [anywhere] * 5 + [vmem] * 2,
        out_specs=(vmem, vmem),
        scratch_shapes=[
            pltpu.VMEM((LEAVES * LEAF, LEAF), BF16),
            pltpu.VMEM((32, 16 * CHUNK), BF16),
            pltpu.VMEM((R, LEAVES * LEAF), F32),
            pltpu.VMEM((LEAVES, R, R), F32),
            pltpu.VMEM((1, R, R), F32),
            pltpu.VMEM((5, 32, WIDE), BF16),
            pltpu.VMEM((HELD, 32, WIDE), BF16),
            pltpu.VMEM((ROW, 32, 256), BF16),
            pltpu.VMEM((32, 256), BF16),
            pltpu.VMEM((ROW, 32, 256), BF16),
            pltpu.VMEM((32, 256), BF16),
            pltpu.VMEM((ROW, 32, 256), BF16),
            eight, plane, rows, eight,
            rows, eight, plane, rows, eight,
            pltpu.VMEM((2, 4 * LEAVES, 128), F32),
            pltpu.VMEM((LEAF - 32, 32 * HELD), BF16),
            pltpu.VMEM((WIDE, LEAF), BF16),
            pltpu.VMEM((LEAF, WIDE), BF16),
            pltpu.VMEM((LEAF, LEAF), BF16),
            pltpu.VMEM((24 * LEAVES, 64), F32),
            pltpu.VMEM((3 * LEAVES, 16, 128), BF16),
            pltpu.VMEM((3 * LEAVES, 8, 128), F32),
            pltpu.VMEM((LEAVES, 128 * NEARL, 1024), BF16),
            pltpu.VMEM((128, 128), F32),
            pltpu.VMEM((128, 128), F32),
            pltpu.VMEM((R, R, 128), F32),
            pltpu.VMEM((8 * R, 128), F32),
            sems((5,)),
            sems((2 * REACH,)), sems((2 * REACH,)),
            sems((3, ROW - 1)), sems((3, ROW - 1)),
            sems((3, ROW - 1)), sems((3, ROW - 1)),
            sems((3, ROW - 1)), sems((3, ROW - 1)),
            sems((2,)), sems((2,)),
        ],
        compiler_params=pltpu.CompilerParams(
            collective_id=0, has_side_effects=True, vmem_limit_bytes=60 << 20
        ),
    )(
        near_blocks, leaf_coords, near_leaves.T, orbitals, density_rows, leaf_basis, leaf_transfer,
        dev_transfer, dev_far, group_far,
    )
    return (density.reshape(-1), hartree.reshape(-1))


def solution(mesh):
    in_specs = (
        P(("group", "dom"), None),
        P(("group", "dom"), None),
        P(("group", "dom"), None),
        P(None, ("group", "dom")),
        P(("group", "dom"), None),
        P(None, ("group", "dom")),
        P(("group", "dom"), None, None),
        P(("group", "dom"), None, None),
        P(("group", "dom"), None),
        P("group", None),
    )
    out_specs = (P(("group", "dom")), P(("group", "dom")))
    return jax.shard_map(local, mesh=mesh, in_specs=in_specs, out_specs=out_specs, check_vma=False)
```

```python
import functools
import math

import jax
import jax.numpy as jnp
from jax import lax
from jax.experimental import pallas as pl
from jax.experimental.pallas import tpu as pltpu
from jax.sharding import PartitionSpec as P

SIDE = 8
LEAF = 512
CHEB = 4
R = 64
BW = 16
NEAR_B = 32
REACH = 8
LEAVES = 6
NEARL = 3
N_DOM = 64
N_GROUP = 8
ROW = 8
FAR_FIRST = (4, 3, 5, 2, 6, 1, 7)
CHUNK = 128
HELD = 2 * REACH + 1
WIDE = 6 * CHUNK

vol_weight = 0.1
MESH = pl.DeviceIdType.MESH
F32 = jnp.float32
BF16 = jnp.bfloat16
CHEB_X = [math.cos((2 * a + 1) * math.pi / (2 * CHEB)) for a in range(CHEB)]


def lanes(start, size):
    return pl.ds(pl.multiple_of(start, size), size)


def remote(src, dst, send, recv, device):
    return pltpu.make_async_remote_copy(
        src_ref=src, dst_ref=dst, send_sem=send, recv_sem=recv, device_id=device, device_id_type=MESH
    )


def signal(barrier, device):
    pl.semaphore_signal(barrier, inc=1, device_id=device, device_id_type=MESH)


def choose(pieces, index):
    piece = pieces[0]
    for s in range(1, len(pieces)):
        piece = jnp.where(index == s, pieces[s], piece)
    return piece


def eye64():
    return lax.broadcasted_iota(jnp.int32, (R, R), 0) == lax.broadcasted_iota(jnp.int32, (R, R), 1)


def to_column(row):
    return jnp.sum(jnp.where(eye64(), row, 0.0), axis=1, keepdims=True)


def to_row(column):
    return jnp.sum(jnp.where(eye64(), column, 0.0), axis=0, keepdims=True)


def split(value):
    high = value.astype(BF16)
    return high, (value - high.astype(F32)).astype(BF16)


def iota(shape, dim):
    return lax.broadcasted_iota(jnp.int32, shape, dim)


def first_and_last(coords, d):
    first = last = coords[d, 0]
    for t in range(1, LEAVES):
        first = jnp.minimum(first, coords[d, t])
        last = jnp.maximum(last, coords[d, t])
    return first, last


def spread(index, shape):
    value = jnp.full(shape, CHEB_X[0], F32)
    for a in range(1, CHEB):
        value = jnp.where(index == a, CHEB_X[a], value)
    return value


def kernel(
    near_h, coords_h, near_leaves_h, group_far_h, dev_far_h,
    orbitals_h, rows_h, basis_h, transfer_h, dev_transfer_h,
    rho_h, out_h, zero_h,
    near, coords, near_leaves, group_far, dev_far,
    orbitals, rows, basis, transfer, dev_transfer, rho, out, zero,
    stage, window, first, passed, second, kept, hot_rows,
    place, places, mom_mine, mom_row, mom_all, mom_total, mom_groups,
    halo, pick_rows, pick_columns, chosen, local_matrix, folded,
    rho_rows, sources, spots, tables, far_rows, far_bounds, partial,
    load_sem, store_sem, w_send, w_recv, h_send, h_recv, u_send, u_recv, e_send, e_recv,
):
    me = lax.axis_index("dom")
    group = lax.axis_index("group")
    y, j = me // ROW, me % ROW
    offsets = [s * o for o in range(REACH, 0, -1) for s in (1, -1)]
    row_peers = [{"dom": y * ROW + (j + d) % ROW} for d in FAR_FIRST]
    column_peers = [{"dom": (me + d * ROW) % N_DOM} for d in FAR_FIRST]
    group_peers = [{"group": (group + d) % N_GROUP} for d in FAR_FIRST]
    peers = [{"dom": (me + o + N_DOM) % N_DOM} for o in offsets]
    peers = peers + [p for d, p in zip(FAR_FIRST, column_peers) if 1 < d < ROW - 1] + group_peers
    barrier = pltpu.get_barrier_semaphore()
    for peer in peers:
        signal(barrier, peer)
    loads = []
    for n, (src, dst) in enumerate(
        (
            (rows_h, rows),
            (near_h, near),
            (coords_h, coords),
            (near_leaves_h, near_leaves),
            (group_far_h, group_far),
            (dev_far_h, dev_far),
            (orbitals_h, orbitals),
            (basis_h, basis),
            (transfer_h, transfer),
            (dev_transfer_h, dev_transfer),
        )
    ):
        loads.append(pltpu.make_async_copy(src, dst, load_sem.at[n]))
    for copy in loads[:6]:
        copy.start()

    def send_all(src, dst, sends, recvs, phase, targets):
        copies = []
        for d, peer in enumerate(targets):
            copy = remote(src, dst, sends.at[phase, d], recvs.at[phase, d], peer)
            copy.start()
            copies.append(copy)
        return copies

    def arrived(copies):
        for copy in copies:
            copy.wait_recv()

    loads[0].wait()
    loads[1].wait()
    hot = near[0, 0] // 2
    base = (me + N_DOM - REACH) // 4
    shared = choose([rows[:, c * CHUNK : (c + 1) * CHUNK] for c in range(16)], hot // 4)
    for kk in range(5):
        for c in range(5):
            chunk = (base + kk + c - 2) % 16
            stage[kk, :, c * CHUNK : (c + 1) * CHUNK] = rows[:, lanes(chunk * CHUNK, CHUNK)]
        stage[kk, :, 5 * CHUNK :] = shared
    window[REACH] = stage[2]
    first[j] = rows[:, lanes(j * 256, 256)]
    loads[2].wait()
    lane = iota((1, 128), 1)
    packed = jnp.zeros((1, 128), jnp.int32)
    for d in range(3):
        low, high = first_and_last(coords, d)
        packed = jnp.where(lane == d, low, packed)
        packed = jnp.where(lane == 3 + d, high, packed)
        for t in range(LEAVES):
            packed = jnp.where(lane == 8 + 3 * t + d, coords[d, t], packed)
    place[...] = packed.astype(F32)
    places[1] = place[...]
    pl.semaphore_wait(barrier, len(peers))

    hot_a = []
    for n, d in enumerate(FAR_FIRST):
        to = (j + d) % ROW
        copy = remote(
            rows.at[:, lanes(to * 256, 256)], first.at[j], h_send.at[0, n], h_recv.at[0, n], row_peers[n]
        )
        copy.start()
        hot_a.append(copy)
    wide = []
    for n, o in enumerate(offsets):
        kk = (me + o + N_DOM) // 4 - base
        copy = remote(stage.at[kk], window.at[REACH - o], w_send.at[n], w_recv.at[n], peers[n])
        copy.start()
        wide.append(copy)
    around = [(me + N_DOM - 1) % N_DOM, me, (me + 1) % N_DOM]
    beside = [
        remote(place, places.at[0], e_send.at[2], e_recv.at[2], {"dom": around[2]}),
        remote(place, places.at[2], e_send.at[3], e_recv.at[3], {"dom": around[0]}),
    ]
    for copy in beside + loads[6:]:
        copy.start()

    gap = iota((BW, 640), 1) - iota((BW, 640), 0)
    for k in range(2, NEAR_B):
        block = near[0, k]
        start = (block // 2 - me + REACH + N_DOM) % N_DOM * 32 + block % 2 * BW
        part = jnp.where(gap == start, 1.0, 0.0)[:, : 32 * HELD]
        pick_rows[(k - 2) * BW : (k - 1) * BW, :] = part.astype(BF16)
    wide_lane = iota((1, LEAF), 1)
    start = jnp.zeros((1, LEAF), jnp.int32)
    for k in range(NEAR_B):
        block = near[0, k]
        chunk = 5 if k < 2 else (block // 8 - me // 4 + 18) % 16
        start = jnp.where(wide_lane // BW == k, chunk * CHUNK + block % 8 * BW, start)
    start = start + wide_lane % BW
    pick = jnp.where(iota((WIDE, LEAF), 0) == start, 1.0, 0.0)
    pick_columns[...] = pick.astype(BF16)

    arrived(hot_a)
    piece = choose([first[s] for s in range(ROW)], hot % ROW)
    passed[...] = piece
    second[y] = piece
    hot_b = send_all(passed, second.at[y], h_send, h_recv, 1, column_peers)
    arrived(hot_b)
    piece = choose([second[s] for s in range(ROW)], hot // ROW)
    kept[...] = piece
    hot_rows[j] = piece
    hot_c = send_all(kept, hot_rows.at[j], h_send, h_recv, 2, row_peers)
    loads[3].wait()
    arrived(beside)
    for s in range(3):
        held = places[s]
        for t in range(LEAVES):
            for d in range(3):
                k = 8 + 3 * t + d
                spots[s * LEAVES + t, d : d + 1, :] = jnp.broadcast_to(held[:, k : k + 1], (1, 128))
    q = iota((64, 128), 0)
    p = iota((64, 128), 1) % 64
    gap_y = (p // 8 - q // 8).astype(F32)
    gap_z = (p % 8 - q % 8).astype(F32)
    step = (2 * iota((8, 128), 0) + iota((8, 128), 1) // 64 - 7).astype(F32)

    def build(t, carry):
        here = spots[LEAVES + t]
        for n in range(NEARL):
            w = near_leaves[n, t]
            shift = SIDE * (here - spots[w])
            x = step + shift[0:1, :]
            yy, zz = gap_y + shift[1:2, :], gap_z + shift[2:3, :]
            x, flat = x * x, yy * yy + zz * zz + 1.0
            for i in range(8):
                high, low = split(lax.rsqrt(flat + x[i : i + 1, :]))
                tables[t, 128 * n : 128 * n + 64, 128 * i : 128 * i + 128] = high
                tables[t, 128 * n + 64 : 128 * n + 128, 128 * i : 128 * i + 128] = low
        return carry

    lax.fori_loop(0, LEAVES, build, 0)

    for copy in loads[4:]:
        copy.wait()
    arrived(wide)
    held = window[...].reshape(32 * HELD, WIDE)
    chosen[...] = jnp.dot(pick_rows[...], held, preferred_element_type=F32).astype(BF16)
    matrix = jnp.dot(chosen[...], pick_columns[...], preferred_element_type=F32)
    local_matrix[0:32, :] = jnp.zeros((32, LEAF), BF16)
    local_matrix[32:, :] = matrix.astype(BF16)

    def window_density(t, carry):
        here = pl.ds(pl.multiple_of(t * LEAF, LEAF), LEAF)
        values = orbitals[here, :]
        product = jnp.dot(values, local_matrix[...], preferred_element_type=F32)
        product = product * values.astype(F32)
        folded[here, :] = (product[:, :128] + product[:, 128:256]) + (
            product[:, 256:384] + product[:, 384:]
        )
        return carry

    lax.fori_loop(0, LEAVES, window_density, 0)

    arrived(hot_c)
    parts = []
    for c in range(5):
        chunk = (me // 4 + 14 + c) % 16
        parts.append(hot_rows[chunk // 2, :, lanes(chunk % 2 * CHUNK, CHUNK)])
    options = [hot_rows[a, :, b * CHUNK : (b + 1) * CHUNK] for a in range(ROW) for b in range(2)]
    parts.append(choose(options, hot // 4))
    matrix = jnp.dot(
        jnp.concatenate(parts, axis=1), pick_columns[...], preferred_element_type=F32
    )
    matrix = jnp.concatenate([matrix, jnp.zeros((96, LEAF), F32)], axis=0).astype(BF16)

    total = jnp.zeros((1, R), F32)
    for t in range(LEAVES):
        here = slice(t * LEAF, (t + 1) * LEAF)
        values = orbitals[here, :]
        product = lax.dot_general(
            values, matrix, (((1,), (1,)), ((), ())), preferred_element_type=F32
        )
        product = product * values[:, :128].astype(F32) + folded[here, :]
        dense = jnp.sum(product.T, axis=0, keepdims=True)
        for i in range(4):
            rho[t * 4 + i : t * 4 + i + 1, :] = dense[:, i * 128 : (i + 1) * 128]
        leaf_moments = jnp.sum(basis[:, here] * dense, axis=1, keepdims=True)
        total = total + jnp.sum(transfer[t] * leaf_moments, axis=0, keepdims=True)
    mine = total
    edge = [
        remote(rho, halo.at[0], e_send.at[0], e_recv.at[0], {"dom": around[2]}),
        remote(rho, halo.at[1], e_send.at[1], e_recv.at[1], {"dom": around[0]}),
    ]
    upward = jnp.sum(dev_transfer[0] * to_column(mine), axis=0, keepdims=True)
    mom_mine[0:1, :] = jnp.concatenate([mine, upward], axis=1)
    mom_mine[1:2, :] = place[...]
    mom_row[j] = mom_mine[...]
    mom_a = send_all(mom_mine, mom_row.at[j], u_send, u_recv, 0, row_peers)
    for copy in edge:
        copy.start()
    rho_store = pltpu.make_async_copy(rho, rho_h, store_sem.at[0])
    rho_store.start()
    zero[...] = jnp.zeros_like(zero)
    zero_store = pltpu.make_async_copy(zero, zero_h, store_sem.at[2])
    zero_store.start()
    arrived(mom_a)
    mom_all[y] = mom_row[...]
    mom_b = send_all(mom_row, mom_all.at[y], u_send, u_recv, 1, column_peers)

    arrived(edge)
    inside = [jnp.where(me > 0, 1.0, 0.0), 1.0, jnp.where(me < N_DOM - 1, 1.0, 0.0)]
    for s, held in enumerate((halo[0], rho[...], halo[1])):
        held = held * inside[s]
        rho_rows[pl.ds(48 * s, 24, stride=2), :] = held[:, :64]
        rho_rows[pl.ds(48 * s + 1, 24, stride=2), :] = held[:, 64:]
    for w in range(3 * LEAVES):
        high, low = split(rho_rows[8 * w : 8 * w + 8, :])
        sources[w] = jnp.concatenate(
            [jnp.concatenate([high, high], axis=1), jnp.concatenate([low, low], axis=1)], axis=0
        )

    def one_near(t, carry):
        lhs = jnp.concatenate([sources[near_leaves[n, t]] for n in range(NEARL)], axis=1)
        both = jnp.dot(lhs, tables[t], preferred_element_type=F32)
        both = both[:8] + both[8:]
        value = jnp.zeros((1, LEAF), F32)
        for qx in range(SIDE):
            value = value + both[qx : qx + 1, (7 - qx) * 64 : (7 - qx) * 64 + LEAF]
        for i in range(4):
            out[pl.ds(4 * t + i, 1), :] = value[:, 128 * i : 128 * i + 128] * vol_weight
        return carry

    lax.fori_loop(0, LEAVES, one_near, 0)

    arrived(mom_b)
    sums, low, high = jnp.zeros((2, 128), F32), mom_all[0, 0], mom_all[0, 0]
    for a in range(ROW):
        for b in range(ROW):
            value = mom_all[a, b]
            sums, low, high = sums + value, jnp.minimum(low, value), jnp.maximum(high, value)
    bounds = jnp.where(lane < 3, low[1:2], high[1:2])
    mom_total[0:1, :] = pltpu.roll(sums, 64, 1)[0:1]
    mom_total[1:2, :] = bounds
    mom_groups[group] = mom_total[...]
    mom_c = send_all(mom_total, mom_groups.at[group], u_send, u_recv, 2, group_peers)

    far_rows[...] = jnp.zeros_like(far_rows)
    far_bounds[...] = jnp.zeros_like(far_bounds)
    for a in range(ROW):
        for b in range(ROW):
            n = a * ROW + b
            far_rows[n : n + 1, :] = mom_all[a, b, 0:1]
            far_bounds[n : n + 1, :] = mom_all[a, b, 1:2]
    mask = jnp.concatenate([dev_far[...], jnp.zeros((1, 128 - N_DOM), jnp.int32)], axis=1)
    weights = far_rows[...].T[:R, :] * mask.astype(F32)
    edges = far_bounds[...].T[:8, :]
    own, other = [], []
    for d in range(3):
        low, high = SIDE * edges[d : d + 1], SIDE * edges[3 + d : 4 + d] + (SIDE - 1)
        own_low, own_high = first_and_last(coords, d)
        own_low = jnp.full((1, 128), SIDE * own_low).astype(F32)
        own_high = jnp.full((1, 128), SIDE * own_high + (SIDE - 1)).astype(F32)
        own.append((0.5 * (own_low + own_high), 0.5 * (own_high - own_low)))
        other.append((0.5 * (low + high), 0.5 * (high - low)))
    sub = iota((8, 128), 0)
    sites = [[c + h * x for x in CHEB_X] for c, h in own]
    xs = [other[0][0] + other[0][1] * x for x in CHEB_X]
    ys = [other[1][0] + other[1][1] * spread(2 * half + sub // 4, (8, 128)) for half in range(2)]
    zs = other[2][0] + other[2][1] * spread(sub % 4, (8, 128))
    dx = [[(s - x) * (s - x) for x in xs] for s in sites[0]]
    dy = [[(s - v) * (s - v) for v in ys] for s in sites[1]]
    dz = [(s - zs) * (s - zs) + 1.0 for s in sites[2]]
    for b in range(CHEB):
        for e in range(CHEB):
            rest = [v + dz[e] for v in dy[b]]
            for a in range(CHEB):
                running = jnp.zeros((8, 128), F32)
                for t in range(8):
                    value = lax.rsqrt(dx[a][t // 2] + rest[t % 2])
                    running = running + value * weights[8 * t : 8 * t + 8]
                r = a * 16 + b * 4 + e
                partial[8 * r : 8 * r + 8, :] = running
    summed = partial[pl.ds(0, R, stride=8), :]
    for k in range(1, 8):
        summed = summed + partial[pl.ds(k, R, stride=8), :]
    dev_local = jnp.sum(summed, axis=1, keepdims=True)
    node = iota((R, 128), 0)
    point = iota((1, 128), 1) % 64
    own_nodes, far_steps = [], []
    for d, scale in enumerate((16, 4, 1)):
        own_low, own_high = SIDE * bounds[:, d : d + 1], SIDE * bounds[:, 3 + d : 4 + d] + (SIDE - 1)
        centre, half = 0.5 * (own_low + own_high), 0.5 * (own_high - own_low)
        own_nodes.append(centre + half * spread(node // scale % 4, (R, 128)))
        far_steps.append(spread(point // scale % 4, (1, 128)))

    arrived(mom_c)
    left = lane < R
    summed = jnp.zeros((R, 128), F32)
    for i in range(N_GROUP // 2):
        one, two = mom_groups[2 * i], mom_groups[2 * i + 1]
        square = jnp.full((R, 128), 1.0, F32)
        for d in range(3):
            low = SIDE * jnp.where(left, one[1:2, d : d + 1], two[1:2, d : d + 1])
            high = jnp.where(left, one[1:2, 3 + d : 4 + d], two[1:2, 3 + d : 4 + d])
            high = SIDE * high + (SIDE - 1)
            gap = own_nodes[d] - (0.5 * (low + high) + 0.5 * (high - low) * far_steps[d])
            square = square + gap * gap
        mask = jnp.where(left, group_far[0, 2 * i], group_far[0, 2 * i + 1]).astype(F32)
        weight = jnp.concatenate([one[0:1, :R], two[0:1, :R]], axis=1) * mask
        summed = summed + lax.rsqrt(square) * weight
    group_local = to_row(jnp.sum(summed, axis=1, keepdims=True))
    dev_total = dev_local + jnp.sum(dev_transfer[0] * group_local, axis=1, keepdims=True)
    dev_total = to_row(dev_total * vol_weight)
    for t in range(LEAVES):
        leaf_local = jnp.sum(transfer[t] * dev_total, axis=1, keepdims=True)
        far = jnp.sum(basis[:, t * LEAF : (t + 1) * LEAF] * leaf_local, axis=0, keepdims=True)
        for i in range(4):
            out[4 * t + i : 4 * t + i + 1, :] += far[:, 128 * i : 128 * i + 128]
    out_store = pltpu.make_async_copy(out, out_h, store_sem.at[1])
    out_store.start()
    for copy in hot_a + hot_b + hot_c + wide + beside + mom_a + mom_b + mom_c + edge:
        copy.wait_send()
    rho_store.wait()
    zero_store.wait()
    out_store.wait()


def local(
    orbitals, density_rows, near_blocks, leaf_coords, near_leaves, leaf_basis, leaf_transfer,
    dev_transfer, dev_far, group_far,
):
    anywhere = pl.BlockSpec(memory_space=pl.ANY)
    rows = pltpu.VMEM((1, 128), F32)
    pair = pltpu.VMEM((2, 128), F32)
    eight = pltpu.VMEM((ROW, 2, 128), F32)
    plane = pltpu.VMEM((ROW, ROW, 2, 128), F32)
    slab = pltpu.VMEM((4 * LEAVES, 128), F32)
    sems = pltpu.SemaphoreType.DMA
    density, hartree, zero = pl.pallas_call(
        kernel,
        out_shape=(jax.ShapeDtypeStruct((4 * LEAVES, 128), F32),) * 3,
        in_specs=[anywhere] * 10,
        out_specs=(anywhere,) * 3,
        scratch_shapes=[
            pltpu.SMEM((1, NEAR_B), jnp.int32),
            pltpu.SMEM((3, LEAVES), jnp.int32),
            pltpu.SMEM((NEARL, LEAVES), jnp.int32),
            pltpu.SMEM((1, N_GROUP), jnp.int32),
            pltpu.VMEM((1, N_DOM), jnp.int32),
            pltpu.VMEM((LEAVES * LEAF, LEAF), BF16),
            pltpu.VMEM((32, 16 * CHUNK), BF16),
            pltpu.VMEM((R, LEAVES * LEAF), F32),
            pltpu.VMEM((LEAVES, R, R), F32),
            pltpu.VMEM((1, R, R), F32),
            slab, slab, slab,
            pltpu.VMEM((5, 32, WIDE), BF16),
            pltpu.VMEM((HELD, 32, WIDE), BF16),
            pltpu.VMEM((ROW, 32, 256), BF16),
            pltpu.VMEM((32, 256), BF16),
            pltpu.VMEM((ROW, 32, 256), BF16),
            pltpu.VMEM((32, 256), BF16),
            pltpu.VMEM((ROW, 32, 256), BF16),
            rows, pltpu.VMEM((3, 1, 128), F32), pair, eight, plane, pair, eight,
            pltpu.VMEM((2, 4 * LEAVES, 128), F32),
            pltpu.VMEM((LEAF - 32, 32 * HELD), BF16),
            pltpu.VMEM((WIDE, LEAF), BF16),
            pltpu.VMEM((LEAF - 32, WIDE), BF16),
            pltpu.VMEM((LEAF, LEAF), BF16),
            pltpu.VMEM((LEAVES * LEAF, 128), F32),
            pltpu.VMEM((24 * LEAVES, 64), F32),
            pltpu.VMEM((3 * LEAVES, 16, 128), BF16),
            pltpu.VMEM((3 * LEAVES, 8, 128), F32),
            pltpu.VMEM((LEAVES, 128 * NEARL, 1024), BF16),
            pltpu.VMEM((128, 128), F32),
            pltpu.VMEM((128, 128), F32),
            pltpu.VMEM((8 * R, 128), F32),
            sems((10,)), sems((3,)),
            sems((2 * REACH,)), sems((2 * REACH,)),
            sems((3, ROW - 1)), sems((3, ROW - 1)),
            sems((3, ROW - 1)), sems((3, ROW - 1)),
            sems((4,)), sems((4,)),
        ],
        compiler_params=pltpu.CompilerParams(
            collective_id=0, has_side_effects=True, vmem_limit_bytes=60 << 20
        ),
    )(
        near_blocks, leaf_coords, near_leaves.T, group_far, dev_far, orbitals, density_rows,
        leaf_basis, leaf_transfer, dev_transfer,
    )
    return ((density + zero).reshape(-1), (hartree + zero).reshape(-1))


def solution(mesh):
    in_specs = (
        P(("group", "dom"), None),
        P(("group", "dom"), None),
        P(("group", "dom"), None),
        P(None, ("group", "dom")),
        P(("group", "dom"), None),
        P(None, ("group", "dom")),
        P(("group", "dom"), None, None),
        P(("group", "dom"), None, None),
        P(("group", "dom"), None),
        P("group", None),
    )
    out_specs = (P(("group", "dom")), P(("group", "dom")))
    return jax.shard_map(local, mesh=mesh, in_specs=in_specs, out_specs=out_specs, check_vma=False)
```

```python
import functools
import math

import jax
import jax.numpy as jnp
from jax import lax
from jax.experimental import pallas as pl
from jax.experimental.pallas import tpu as pltpu
from jax.sharding import PartitionSpec as P

SIDE = 8
LEAF = 512
CHEB = 4
R = 64
BW = 16
NEAR_B = 32
REACH = 8
LEAVES = 6
NEARL = 3
N_DOM = 64
N_GROUP = 8
ROW = 8
FAR_FIRST = (4, 3, 5, 2, 6, 1, 7)
CHUNK = 128
SPAN = REACH // 2
HELD = 2 * (2 * SPAN + 1)
WIDE = 6 * CHUNK

vol_weight = 0.1
MESH = pl.DeviceIdType.MESH
F32 = jnp.float32
BF16 = jnp.bfloat16
CHEB_X = [math.cos((2 * a + 1) * math.pi / (2 * CHEB)) for a in range(CHEB)]


def lanes(start, size):
    return pl.ds(pl.multiple_of(start, size), size)


def remote(src, dst, send, recv, device):
    return pltpu.make_async_remote_copy(
        src_ref=src, dst_ref=dst, send_sem=send, recv_sem=recv, device_id=device, device_id_type=MESH
    )


def signal(barrier, device):
    pl.semaphore_signal(barrier, inc=1, device_id=device, device_id_type=MESH)


def choose(pieces, index):
    piece = pieces[0]
    for s in range(1, len(pieces)):
        piece = jnp.where(index == s, pieces[s], piece)
    return piece


def eye64():
    return lax.broadcasted_iota(jnp.int32, (R, R), 0) == lax.broadcasted_iota(jnp.int32, (R, R), 1)


def to_column(row):
    return jnp.sum(jnp.where(eye64(), row, 0.0), axis=1, keepdims=True)


def to_row(column):
    return jnp.sum(jnp.where(eye64(), column, 0.0), axis=0, keepdims=True)


def split(value):
    high = value.astype(BF16)
    return high, (value - high.astype(F32)).astype(BF16)


def iota(shape, dim):
    return lax.broadcasted_iota(jnp.int32, shape, dim)


def first_and_last(coords, d):
    first = last = coords[d, 0]
    for t in range(1, LEAVES):
        first = jnp.minimum(first, coords[d, t])
        last = jnp.maximum(last, coords[d, t])
    return first, last


def spread(index, shape):
    value = jnp.full(shape, CHEB_X[0], F32)
    for a in range(1, CHEB):
        value = jnp.where(index == a, CHEB_X[a], value)
    return value


def kernel(
    near_h, coords_h, near_leaves_h, group_far_h, dev_far_h,
    orbitals_h, rows_h, basis_h, transfer_h, dev_transfer_h,
    rho_h, out_h, zero_h,
    near, coords, near_leaves, group_far, dev_far,
    orbitals, rows, basis, transfer, dev_transfer, rho, out, zero,
    stage, window, first, passed, second, kept, hot_rows,
    place, places, mom_mine, mom_row, bundle, mom_all, mom_total, mom_groups,
    halo, pick_rows, pick_columns, chosen, local_matrix, folded,
    rho_rows, sources, spots, tables, far_rows, partial,
    load_sem, store_sem, w_send, w_recv, h_send, h_recv, u_send, u_recv, e_send, e_recv,
):
    me = lax.axis_index("dom")
    group = lax.axis_index("group")
    y, j = me // ROW, me % ROW
    core, chip = me % 2, me // 2
    chips = [s * o for o in range(SPAN, 0, -1) for s in (1, -1)]
    sibling = {"dom": me + 1 - 2 * core}
    row_peers = [{"dom": y * ROW + (j + d) % ROW} for d in FAR_FIRST]
    column_peers = [{"dom": (me + d * ROW) % N_DOM} for d in FAR_FIRST]
    group_peers = [{"group": (group + d) % N_GROUP} for d in FAR_FIRST]
    window_peers = [{"dom": (me + 2 * o + N_DOM) % N_DOM} for o in chips]
    around = [(me + N_DOM - 1) % N_DOM, me, (me + 1) % N_DOM]
    peers = window_peers + row_peers + [{"dom": around[0]}, {"dom": around[2]}]
    peers = peers + [p for d, p in zip(FAR_FIRST, column_peers) if 1 < d < ROW - 1] + group_peers
    barrier = pltpu.get_barrier_semaphore()
    for peer in peers:
        signal(barrier, peer)
    loads = []
    for n, (src, dst) in enumerate(
        (
            (rows_h, rows),
            (near_h, near),
            (coords_h, coords),
            (near_leaves_h, near_leaves),
            (group_far_h, group_far),
            (dev_far_h, dev_far),
            (orbitals_h, orbitals),
            (basis_h, basis),
            (transfer_h, transfer),
            (dev_transfer_h, dev_transfer),
        )
    ):
        loads.append(pltpu.make_async_copy(src, dst, load_sem.at[n]))
    for copy in loads[:6]:
        copy.start()

    def send_all(src, dst, sends, recvs, phase, targets):
        copies = []
        for d, peer in enumerate(targets):
            copy = remote(src, dst, sends.at[phase, d], recvs.at[phase, d], peer)
            copy.start()
            copies.append(copy)
        return copies

    def arrived(copies):
        for copy in copies:
            copy.wait_recv()

    loads[0].wait()
    loads[1].wait()
    hot = near[0, 0] // 2
    base = (me + N_DOM - REACH) // 4
    shared = choose([rows[:, c * CHUNK : (c + 1) * CHUNK] for c in range(16)], hot // 4)
    for kk in range(5):
        for c in range(5):
            chunk = (base + kk + c - 2) % 16
            stage[kk, :, c * CHUNK : (c + 1) * CHUNK] = rows[:, lanes(chunk * CHUNK, CHUNK)]
        stage[kk, :, 5 * CHUNK :] = shared
    window[2 * SPAN + core] = stage[2]
    first[j] = rows[:, lanes(j * 256, 256)]
    loads[2].wait()
    lane = iota((1, 128), 1)
    packed = jnp.zeros((1, 128), jnp.int32)
    for d in range(3):
        low, high = first_and_last(coords, d)
        packed = jnp.where(lane == d, low, packed)
        packed = jnp.where(lane == 3 + d, high, packed)
        for t in range(LEAVES):
            packed = jnp.where(lane == 8 + 3 * t + d, coords[d, t], packed)
    place[...] = packed.astype(F32)
    places[1] = place[...]
    pl.semaphore_wait(barrier, len(peers))

    hot_a = []
    for n, d in enumerate(FAR_FIRST):
        to = (j + d) % ROW
        copy = remote(
            rows.at[:, lanes(to * 256, 256)], first.at[j], h_send.at[0, n], h_recv.at[0, n], row_peers[n]
        )
        copy.start()
        hot_a.append(copy)
    wide = []
    for n, o in enumerate(chips):
        kk = (me + 2 * o + N_DOM) // 4 - base
        slot = 2 * (SPAN - o) + core
        copy = remote(stage.at[kk], window.at[slot], w_send.at[0, n], w_recv.at[0, n], window_peers[n])
        copy.start()
        wide.append(copy)
    own = window.at[2 * SPAN + core]
    shared_out = [remote(own, own, w_send.at[1, 8], w_recv.at[1, 8], sibling)]
    shared_out[0].start()
    beside = [
        remote(place, places.at[0], e_send.at[2], e_recv.at[2], {"dom": around[2]}),
        remote(place, places.at[2], e_send.at[3], e_recv.at[3], {"dom": around[0]}),
    ]
    for copy in beside + loads[6:]:
        copy.start()

    arrived(hot_a)
    piece = choose([first[s] for s in range(ROW)], hot % ROW)
    passed[...] = piece
    second[y] = piece
    hot_b = send_all(passed, second.at[y], h_send, h_recv, 1, column_peers)
    gap = iota((BW, 640), 1) - iota((BW, 640), 0)
    for k in range(2, NEAR_B):
        block = near[0, k]
        slot = (block // 4 - chip + SPAN + N_DOM // 2) % (N_DOM // 2) * 2 + block // 2 % 2
        start = slot * 32 + block % 2 * BW
        part = jnp.where(gap == start, 1.0, 0.0)[:, : 32 * HELD]
        pick_rows[(k - 2) * BW : (k - 1) * BW, :] = part.astype(BF16)
    wide_lane = iota((1, LEAF), 1)
    start = jnp.zeros((1, LEAF), jnp.int32)
    for k in range(NEAR_B):
        block = near[0, k]
        chunk = 5 if k < 2 else (block // 8 - me // 4 + 18) % 16
        start = jnp.where(wide_lane // BW == k, chunk * CHUNK + block % 8 * BW, start)
    start = start + wide_lane % BW
    pick = jnp.where(iota((WIDE, LEAF), 0) == start, 1.0, 0.0)
    pick_columns[...] = pick.astype(BF16)

    arrived(hot_b)
    piece = choose([second[s] for s in range(ROW)], hot // ROW)
    kept[...] = piece
    hot_rows[j] = piece
    hot_c = send_all(kept, hot_rows.at[j], h_send, h_recv, 2, row_peers)
    loads[3].wait()
    arrived(beside)
    for s in range(3):
        held = places[s]
        for t in range(LEAVES):
            for d in range(3):
                k = 8 + 3 * t + d
                spots[s * LEAVES + t, d : d + 1, :] = jnp.broadcast_to(held[:, k : k + 1], (1, 128))
    q = iota((64, 128), 0)
    p = iota((64, 128), 1) % 64
    gap_y = (p // 8 - q // 8).astype(F32)
    gap_z = (p % 8 - q % 8).astype(F32)
    step = (2 * iota((8, 128), 0) + iota((8, 128), 1) // 64 - 7).astype(F32)

    def build(t, carry):
        here = spots[LEAVES + t]
        for n in range(NEARL):
            w = near_leaves[n, t]
            shift = SIDE * (here - spots[w])
            x = step + shift[0:1, :]
            yy, zz = gap_y + shift[1:2, :], gap_z + shift[2:3, :]
            x, flat = x * x, yy * yy + zz * zz + 1.0
            for i in range(8):
                high, low = split(lax.rsqrt(flat + x[i : i + 1, :]))
                tables[t, 128 * n : 128 * n + 64, 128 * i : 128 * i + 128] = high
                tables[t, 128 * n + 64 : 128 * n + 128, 128 * i : 128 * i + 128] = low
        return carry

    lax.fori_loop(0, LEAVES, build, 0)

    for copy in loads[4:]:
        copy.wait()
    for n, o in enumerate(chips):
        wide[n].wait_recv()
        piece = window.at[2 * (SPAN - o) + core]
        copy = remote(piece, piece, w_send.at[1, n], w_recv.at[1, n], sibling)
        copy.start()
        shared_out.append(copy)
    arrived(shared_out)
    held = window[...].reshape(32 * HELD, WIDE)
    chosen[...] = jnp.dot(pick_rows[...], held, preferred_element_type=F32).astype(BF16)
    matrix = jnp.dot(chosen[...], pick_columns[...], preferred_element_type=F32)
    local_matrix[0:32, :] = jnp.zeros((32, LEAF), BF16)
    local_matrix[32:, :] = matrix.astype(BF16)

    def window_density(t, carry):
        here = pl.ds(pl.multiple_of(t * LEAF, LEAF), LEAF)
        values = orbitals[here, :]
        product = jnp.dot(values, local_matrix[...], preferred_element_type=F32)
        product = product * values.astype(F32)
        folded[here, :] = (product[:, :128] + product[:, 128:256]) + (
            product[:, 256:384] + product[:, 384:]
        )
        return carry

    lax.fori_loop(0, LEAVES, window_density, 0)

    arrived(hot_c)
    parts = []
    for c in range(5):
        chunk = (me // 4 + 14 + c) % 16
        parts.append(hot_rows[chunk // 2, :, lanes(chunk % 2 * CHUNK, CHUNK)])
    options = [hot_rows[a, :, b * CHUNK : (b + 1) * CHUNK] for a in range(ROW) for b in range(2)]
    parts.append(choose(options, hot // 4))
    matrix = jnp.dot(
        jnp.concatenate(parts, axis=1), pick_columns[...], preferred_element_type=F32
    )
    matrix = jnp.concatenate([matrix, jnp.zeros((96, LEAF), F32)], axis=0).astype(BF16)

    total = jnp.zeros((1, R), F32)
    for t in range(LEAVES):
        here = slice(t * LEAF, (t + 1) * LEAF)
        values = orbitals[here, :]
        product = lax.dot_general(
            values, matrix, (((1,), (1,)), ((), ())), preferred_element_type=F32
        )
        product = product * values[:, :128].astype(F32) + folded[here, :]
        dense = jnp.sum(product.T, axis=0, keepdims=True)
        for i in range(4):
            rho[t * 4 + i : t * 4 + i + 1, :] = dense[:, i * 128 : (i + 1) * 128]
        leaf_moments = jnp.sum(basis[:, here] * dense, axis=1, keepdims=True)
        total = total + jnp.sum(transfer[t] * leaf_moments, axis=0, keepdims=True)
    mine = total
    edge = [
        remote(rho, halo.at[0], e_send.at[0], e_recv.at[0], {"dom": around[2]}),
        remote(rho, halo.at[1], e_send.at[1], e_recv.at[1], {"dom": around[0]}),
    ]
    upward = jnp.sum(dev_transfer[0] * to_column(mine), axis=0, keepdims=True)
    beyond = pltpu.roll(place[...], R, 1)
    mom_mine[0:1, :] = jnp.where(lane < R, jnp.concatenate([mine, mine], axis=1), beyond)
    mom_mine[1:2, :] = jnp.concatenate([upward, upward], axis=1)
    mom_row[j] = mom_mine[...]
    mom_a = send_all(mom_mine, mom_row.at[j], u_send, u_recv, 0, row_peers)
    for copy in edge:
        copy.start()
    rho_store = pltpu.make_async_copy(rho, rho_h, store_sem.at[0])
    rho_store.start()
    zero[...] = jnp.zeros_like(zero)
    zero_store = pltpu.make_async_copy(zero, zero_h, store_sem.at[2])
    zero_store.start()
    arrived(mom_a)
    sums, low, high = jnp.zeros((2, 128), F32), mom_row[0], mom_row[0]
    for b in range(ROW):
        value = mom_row[b]
        bundle[b] = value[0:1]
        sums, low, high = sums + value, jnp.minimum(low, value), jnp.maximum(high, value)
    bounds = jnp.where(lane < R + 3, low[0:1], high[0:1])
    bundle[ROW] = jnp.where(lane < R, sums[1:2], bounds)
    mom_all[y] = bundle[...]
    mom_b = send_all(bundle, mom_all.at[y], u_send, u_recv, 1, column_peers)

    arrived(edge)
    inside = [jnp.where(me > 0, 1.0, 0.0), 1.0, jnp.where(me < N_DOM - 1, 1.0, 0.0)]
    for s, held in enumerate((halo[0], rho[...], halo[1])):
        held = held * inside[s]
        rho_rows[pl.ds(48 * s, 24, stride=2), :] = held[:, :64]
        rho_rows[pl.ds(48 * s + 1, 24, stride=2), :] = held[:, 64:]
    for w in range(3 * LEAVES):
        high, low = split(rho_rows[8 * w : 8 * w + 8, :])
        sources[w] = jnp.concatenate(
            [jnp.concatenate([high, high], axis=1), jnp.concatenate([low, low], axis=1)], axis=0
        )

    def one_near(t, carry):
        lhs = jnp.concatenate([sources[near_leaves[n, t]] for n in range(NEARL)], axis=1)
        both = jnp.dot(lhs, tables[t], preferred_element_type=F32)
        both = both[:8] + both[8:]
        value = jnp.zeros((1, LEAF), F32)
        for qx in range(SIDE):
            value = value + both[qx : qx + 1, (7 - qx) * 64 : (7 - qx) * 64 + LEAF]
        for i in range(4):
            out[pl.ds(4 * t + i, 1), :] = value[:, 128 * i : 128 * i + 128] * vol_weight
        return carry

    lax.fori_loop(0, LEAVES, one_near, 0)

    arrived(mom_b)
    sums, low, high = jnp.zeros((1, 128), F32), mom_all[0, ROW], mom_all[0, ROW]
    for a in range(ROW):
        value = mom_all[a, ROW]
        sums, low, high = sums + value, jnp.minimum(low, value), jnp.maximum(high, value)
    bounds = jnp.where(lane < R + 3, low, high)
    mom_total[...] = jnp.where(lane < R, sums, bounds)
    mom_groups[group] = mom_total[...]
    mom_c = send_all(mom_total, mom_groups.at[group], u_send, u_recv, 2, group_peers)

    far_rows[...] = jnp.zeros_like(far_rows)
    for a in range(ROW):
        for b in range(ROW):
            n = a * ROW + b
            far_rows[n : n + 1, :] = mom_all[a, b]
    mask = jnp.concatenate([dev_far[...], jnp.zeros((1, 128 - N_DOM), jnp.int32)], axis=1)
    flipped = far_rows[...].T
    weights, edges = flipped[:R] * mask.astype(F32), flipped[R : R + 8]
    own, other = [], []
    for d in range(3):
        low, high = SIDE * edges[d : d + 1], SIDE * edges[3 + d : 4 + d] + (SIDE - 1)
        own_low, own_high = first_and_last(coords, d)
        own_low = jnp.full((1, 128), SIDE * own_low).astype(F32)
        own_high = jnp.full((1, 128), SIDE * own_high + (SIDE - 1)).astype(F32)
        own.append((0.5 * (own_low + own_high), 0.5 * (own_high - own_low)))
        other.append((0.5 * (low + high), 0.5 * (high - low)))
    sub = iota((8, 128), 0)
    sites = [[c + h * x for x in CHEB_X] for c, h in own]
    xs = [other[0][0] + other[0][1] * x for x in CHEB_X]
    ys = [other[1][0] + other[1][1] * spread(2 * half + sub // 4, (8, 128)) for half in range(2)]
    zs = other[2][0] + other[2][1] * spread(sub % 4, (8, 128))
    dx = [[(s - x) * (s - x) for x in xs] for s in sites[0]]
    dy = [[(s - v) * (s - v) for v in ys] for s in sites[1]]
    dz = [(s - zs) * (s - zs) + 1.0 for s in sites[2]]
    for b in range(CHEB):
        for e in range(CHEB):
            rest = [v + dz[e] for v in dy[b]]
            for a in range(CHEB):
                running = jnp.zeros((8, 128), F32)
                for t in range(8):
                    value = lax.rsqrt(dx[a][t // 2] + rest[t % 2])
                    running = running + value * weights[8 * t : 8 * t + 8]
                r = a * 16 + b * 4 + e
                partial[8 * r : 8 * r + 8, :] = running
    summed = partial[pl.ds(0, R, stride=8), :]
    for k in range(1, 8):
        summed = summed + partial[pl.ds(k, R, stride=8), :]
    dev_local = jnp.sum(summed, axis=1, keepdims=True)
    node = iota((R, 128), 0)
    point = iota((1, 128), 1) % 64
    own_nodes, far_steps = [], []
    for d, scale in enumerate((16, 4, 1)):
        own_low, own_high = SIDE * bounds[:, R + d : R + d + 1], bounds[:, R + 3 + d : R + 4 + d]
        own_high = SIDE * own_high + (SIDE - 1)
        centre, half = 0.5 * (own_low + own_high), 0.5 * (own_high - own_low)
        own_nodes.append(centre + half * spread(node // scale % 4, (R, 128)))
        far_steps.append(spread(point // scale % 4, (1, 128)))

    arrived(mom_c)
    left = lane < R
    summed = jnp.zeros((R, 128), F32)
    for i in range(N_GROUP // 2):
        one, two = mom_groups[2 * i], mom_groups[2 * i + 1]
        square = jnp.full((R, 128), 1.0, F32)
        for d in range(3):
            at, to = slice(R + d, R + d + 1), slice(R + 3 + d, R + 4 + d)
            low = SIDE * jnp.where(left, one[:, at], two[:, at])
            high = jnp.where(left, one[:, to], two[:, to])
            high = SIDE * high + (SIDE - 1)
            gap = own_nodes[d] - (0.5 * (low + high) + 0.5 * (high - low) * far_steps[d])
            square = square + gap * gap
        mask = jnp.where(left, group_far[0, 2 * i], group_far[0, 2 * i + 1]).astype(F32)
        weight = jnp.concatenate([one[:, :R], two[:, :R]], axis=1) * mask
        summed = summed + lax.rsqrt(square) * weight
    group_local = to_row(jnp.sum(summed, axis=1, keepdims=True))
    dev_total = dev_local + jnp.sum(dev_transfer[0] * group_local, axis=1, keepdims=True)
    dev_total = to_row(dev_total * vol_weight)
    for t in range(LEAVES):
        leaf_local = jnp.sum(transfer[t] * dev_total, axis=1, keepdims=True)
        far = jnp.sum(basis[:, t * LEAF : (t + 1) * LEAF] * leaf_local, axis=0, keepdims=True)
        for i in range(4):
            out[4 * t + i : 4 * t + i + 1, :] += far[:, 128 * i : 128 * i + 128]
    out_store = pltpu.make_async_copy(out, out_h, store_sem.at[1])
    out_store.start()
    for copy in hot_a + hot_b + hot_c + wide + shared_out + beside + mom_a + mom_b + mom_c + edge:
        copy.wait_send()
    rho_store.wait()
    zero_store.wait()
    out_store.wait()


def local(
    orbitals, density_rows, near_blocks, leaf_coords, near_leaves, leaf_basis, leaf_transfer,
    dev_transfer, dev_far, group_far,
):
    anywhere = pl.BlockSpec(memory_space=pl.ANY)
    rows = pltpu.VMEM((1, 128), F32)
    slab = pltpu.VMEM((4 * LEAVES, 128), F32)
    sems = pltpu.SemaphoreType.DMA
    density, hartree, zero = pl.pallas_call(
        kernel,
        out_shape=(jax.ShapeDtypeStruct((4 * LEAVES, 128), F32),) * 3,
        in_specs=[anywhere] * 10,
        out_specs=(anywhere,) * 3,
        scratch_shapes=[
            pltpu.SMEM((1, NEAR_B), jnp.int32),
            pltpu.SMEM((3, LEAVES), jnp.int32),
            pltpu.SMEM((NEARL, LEAVES), jnp.int32),
            pltpu.SMEM((1, N_GROUP), jnp.int32),
            pltpu.VMEM((1, N_DOM), jnp.int32),
            pltpu.VMEM((LEAVES * LEAF, LEAF), BF16),
            pltpu.VMEM((32, 16 * CHUNK), BF16),
            pltpu.VMEM((R, LEAVES * LEAF), F32),
            pltpu.VMEM((LEAVES, R, R), F32),
            pltpu.VMEM((1, R, R), F32),
            slab, slab, slab,
            pltpu.VMEM((5, 32, WIDE), BF16),
            pltpu.VMEM((HELD, 32, WIDE), BF16),
            pltpu.VMEM((ROW, 32, 256), BF16),
            pltpu.VMEM((32, 256), BF16),
            pltpu.VMEM((ROW, 32, 256), BF16),
            pltpu.VMEM((32, 256), BF16),
            pltpu.VMEM((ROW, 32, 256), BF16),
            rows,
            pltpu.VMEM((3, 1, 128), F32),
            pltpu.VMEM((2, 128), F32),
            pltpu.VMEM((ROW, 2, 128), F32),
            pltpu.VMEM((ROW + 1, 1, 128), F32),
            pltpu.VMEM((ROW, ROW + 1, 1, 128), F32),
            rows,
            pltpu.VMEM((N_GROUP, 1, 128), F32),
            pltpu.VMEM((2, 4 * LEAVES, 128), F32),
            pltpu.VMEM((LEAF - 32, 32 * HELD), BF16),
            pltpu.VMEM((WIDE, LEAF), BF16),
            pltpu.VMEM((LEAF - 32, WIDE), BF16),
            pltpu.VMEM((LEAF, LEAF), BF16),
            pltpu.VMEM((LEAVES * LEAF, 128), F32),
            pltpu.VMEM((24 * LEAVES, 64), F32),
            pltpu.VMEM((3 * LEAVES, 16, 128), BF16),
            pltpu.VMEM((3 * LEAVES, 8, 128), F32),
            pltpu.VMEM((LEAVES, 128 * NEARL, 1024), BF16),
            pltpu.VMEM((128, 128), F32),
            pltpu.VMEM((8 * R, 128), F32),
            sems((10,)), sems((3,)),
            sems((2, 9)), sems((2, 9)),
            sems((3, ROW - 1)), sems((3, ROW - 1)),
            sems((3, ROW - 1)), sems((3, ROW - 1)),
            sems((4,)), sems((4,)),
        ],
        compiler_params=pltpu.CompilerParams(
            collective_id=0, has_side_effects=True, vmem_limit_bytes=60 << 20
        ),
    )(
        near_blocks, leaf_coords, near_leaves.T, group_far, dev_far, orbitals, density_rows,
        leaf_basis, leaf_transfer, dev_transfer,
    )
    return ((density + zero).reshape(-1), (hartree + zero).reshape(-1))


def solution(mesh):
    in_specs = (
        P(("group", "dom"), None),
        P(("group", "dom"), None),
        P(("group", "dom"), None),
        P(None, ("group", "dom")),
        P(("group", "dom"), None),
        P(None, ("group", "dom")),
        P(("group", "dom"), None, None),
        P(("group", "dom"), None, None),
        P(("group", "dom"), None),
        P("group", None),
    )
    out_specs = (P(("group", "dom")), P(("group", "dom")))
    return jax.shard_map(local, mesh=mesh, in_specs=in_specs, out_specs=out_specs, check_vma=False)
```

```python
import functools
import math

import jax
import jax.numpy as jnp
from jax import lax
from jax.experimental import pallas as pl
from jax.experimental.pallas import tpu as pltpu
from jax.sharding import PartitionSpec as P

SIDE = 8
LEAF = 512
CHEB = 4
R = 64
BW = 16
NEAR_B = 32
REACH = 8
LEAVES = 6
NEARL = 3
N_DOM = 64
N_GROUP = 8
ROW = 8
FAR_FIRST = (4, 3, 5, 2, 6, 1, 7)
CHUNK = 128
SPAN = REACH // 2
HELD = 2 * (2 * SPAN + 1)
WIDE = 6 * CHUNK

vol_weight = 0.1
MESH = pl.DeviceIdType.MESH
F32 = jnp.float32
BF16 = jnp.bfloat16
CHEB_X = [math.cos((2 * a + 1) * math.pi / (2 * CHEB)) for a in range(CHEB)]


def lanes(start, size):
    return pl.ds(pl.multiple_of(start, size), size)


def remote(src, dst, send, recv, device):
    return pltpu.make_async_remote_copy(
        src_ref=src, dst_ref=dst, send_sem=send, recv_sem=recv, device_id=device, device_id_type=MESH
    )


def signal(barrier, device):
    pl.semaphore_signal(barrier, inc=1, device_id=device, device_id_type=MESH)


def choose(pieces, index):
    piece = pieces[0]
    for s in range(1, len(pieces)):
        piece = jnp.where(index == s, pieces[s], piece)
    return piece


def eye64():
    return lax.broadcasted_iota(jnp.int32, (R, R), 0) == lax.broadcasted_iota(jnp.int32, (R, R), 1)


def to_column(row):
    return jnp.sum(jnp.where(eye64(), row, 0.0), axis=1, keepdims=True)


def to_row(column):
    return jnp.sum(jnp.where(eye64(), column, 0.0), axis=0, keepdims=True)


def split(value):
    high = value.astype(BF16)
    return high, (value - high.astype(F32)).astype(BF16)


def iota(shape, dim):
    return lax.broadcasted_iota(jnp.int32, shape, dim)


def first_and_last(coords, d):
    first = last = coords[d, 0]
    for t in range(1, LEAVES):
        first = jnp.minimum(first, coords[d, t])
        last = jnp.maximum(last, coords[d, t])
    return first, last


def spread(index, shape):
    value = jnp.full(shape, CHEB_X[0], F32)
    for a in range(1, CHEB):
        value = jnp.where(index == a, CHEB_X[a], value)
    return value


def kernel(
    near_h, coords_h, near_leaves_h, group_far_h, dev_far_h,
    orbitals_h, rows_h, basis_h, transfer_h, dev_transfer_h,
    rho_h, out_h, zero_h,
    near, coords, near_leaves, group_far, dev_far,
    orbitals, rows, basis, transfer, dev_transfer, rho, out, zero,
    stage, window, first, passed, second, kept, hot_rows,
    place, places, mom_mine, mom_row, bundle, mom_all, mom_total, mom_groups,
    halo, pick_rows, pick_columns, chosen, local_matrix, folded,
    rho_rows, sources, spots, tables, far_rows, partial,
    load_sem, store_sem, w_send, w_recv, h_send, h_recv, u_send, u_recv, e_send, e_recv,
):
    me = lax.axis_index("dom")
    group = lax.axis_index("group")
    y, j = me // ROW, me % ROW
    core, chip = me % 2, me // 2
    chips = [s * o for o in range(SPAN, 0, -1) for s in (1, -1)]
    sibling = {"dom": me + 1 - 2 * core}
    row_peers = [{"dom": y * ROW + (j + d) % ROW} for d in FAR_FIRST]
    column_peers = [{"dom": (me + d * ROW) % N_DOM} for d in FAR_FIRST]
    group_peers = [{"group": (group + d) % N_GROUP} for d in FAR_FIRST]
    window_peers = [{"dom": (me + 2 * o + N_DOM) % N_DOM} for o in chips]
    around = [(me + N_DOM - 1) % N_DOM, me, (me + 1) % N_DOM]
    peers = window_peers + row_peers + [{"dom": around[0]}, {"dom": around[2]}]
    peers = peers + [p for d, p in zip(FAR_FIRST, column_peers) if 1 < d < ROW - 1] + group_peers
    barrier = pltpu.get_barrier_semaphore()
    for peer in peers:
        signal(barrier, peer)
    loads = []
    for n, (src, dst) in enumerate(
        (
            (rows_h, rows),
            (near_h, near),
            (coords_h, coords),
            (near_leaves_h, near_leaves),
            (group_far_h, group_far),
            (dev_far_h, dev_far),
            (orbitals_h, orbitals),
            (basis_h, basis),
            (transfer_h, transfer),
            (dev_transfer_h, dev_transfer),
        )
    ):
        loads.append(pltpu.make_async_copy(src, dst, load_sem.at[n]))
    for copy in loads[:6]:
        copy.start()

    def send_all(src, dst, sends, recvs, phase, targets):
        copies = []
        for d, peer in enumerate(targets):
            copy = remote(src, dst, sends.at[phase, d], recvs.at[phase, d], peer)
            copy.start()
            copies.append(copy)
        return copies

    def arrived(copies):
        for copy in copies:
            copy.wait_recv()

    loads[0].wait()
    loads[1].wait()
    hot = near[0, 0] // 2
    base = (me + N_DOM - REACH) // 4
    shared = choose([rows[:, c * CHUNK : (c + 1) * CHUNK] for c in range(16)], hot // 4)
    for kk in range(5):
        for c in range(5):
            chunk = (base + kk + c - 2) % 16
            stage[kk, :, c * CHUNK : (c + 1) * CHUNK] = rows[:, lanes(chunk * CHUNK, CHUNK)]
        stage[kk, :, 5 * CHUNK :] = shared
    window[2 * SPAN + core] = stage[2]
    first[j] = rows[:, lanes(j * 256, 256)]
    loads[2].wait()
    lane = iota((1, 128), 1)
    packed = jnp.zeros((1, 128), jnp.int32)
    for d in range(3):
        low, high = first_and_last(coords, d)
        packed = jnp.where(lane == d, low, packed)
        packed = jnp.where(lane == 3 + d, high, packed)
        for t in range(LEAVES):
            packed = jnp.where(lane == 8 + 3 * t + d, coords[d, t], packed)
    place[...] = packed.astype(F32)
    places[1] = place[...]
    pl.semaphore_wait(barrier, len(peers))

    hot_a = []
    for n, d in enumerate(FAR_FIRST):
        to = (j + d) % ROW
        copy = remote(
            rows.at[:, lanes(to * 256, 256)], first.at[j], h_send.at[0, n], h_recv.at[0, n], row_peers[n]
        )
        copy.start()
        hot_a.append(copy)
    wide = []
    for n, o in enumerate(chips):
        kk = (me + 2 * o + N_DOM) // 4 - base
        slot = 2 * (SPAN - o) + core
        copy = remote(stage.at[kk], window.at[slot], w_send.at[0, n], w_recv.at[0, n], window_peers[n])
        copy.start()
        wide.append(copy)
    own = window.at[2 * SPAN + core]
    shared_out = [remote(own, own, w_send.at[1, 8], w_recv.at[1, 8], sibling)]
    shared_out[0].start()
    beside = [
        remote(place, places.at[0], e_send.at[2], e_recv.at[2], {"dom": around[2]}),
        remote(place, places.at[2], e_send.at[3], e_recv.at[3], {"dom": around[0]}),
    ]
    for copy in beside + loads[6:]:
        copy.start()

    arrived(hot_a)
    piece = choose([first[s] for s in range(ROW)], hot % ROW)
    passed[...] = piece
    second[y] = piece
    hot_b = send_all(passed, second.at[y], h_send, h_recv, 1, column_peers)
    gap = iota((BW, 640), 1) - iota((BW, 640), 0)
    for k in range(2, NEAR_B):
        block = near[0, k]
        slot = (block // 4 - chip + SPAN + N_DOM // 2) % (N_DOM // 2) * 2 + block // 2 % 2
        start = slot * 32 + block % 2 * BW
        part = jnp.where(gap == start, 1.0, 0.0)[:, : 32 * HELD]
        pick_rows[(k - 2) * BW : (k - 1) * BW, :] = part.astype(BF16)
    wide_lane = iota((1, LEAF), 1)
    start = jnp.zeros((1, LEAF), jnp.int32)
    for k in range(NEAR_B):
        block = near[0, k]
        chunk = 5 if k < 2 else (block // 8 - me // 4 + 18) % 16
        start = jnp.where(wide_lane // BW == k, chunk * CHUNK + block % 8 * BW, start)
    start = start + wide_lane % BW
    pick = jnp.where(iota((WIDE, LEAF), 0) == start, 1.0, 0.0)
    pick_columns[...] = pick.astype(BF16)

    for n, o in enumerate(chips):
        wide[n].wait_recv()
        piece = window.at[2 * (SPAN - o) + core]
        copy = remote(piece, piece, w_send.at[1, n], w_recv.at[1, n], sibling)
        copy.start()
        shared_out.append(copy)
    arrived(hot_b)
    piece = choose([second[s] for s in range(ROW)], hot // ROW)
    kept[...] = piece
    hot_rows[j] = piece
    hot_c = send_all(kept, hot_rows.at[j], h_send, h_recv, 2, row_peers)
    loads[3].wait()
    arrived(beside)
    for s in range(3):
        held = places[s]
        for t in range(LEAVES):
            for d in range(3):
                k = 8 + 3 * t + d
                spots[s * LEAVES + t, d : d + 1, :] = jnp.broadcast_to(held[:, k : k + 1], (1, 128))
    q = iota((64, 128), 0)
    p = iota((64, 128), 1) % 64
    gap_y = (p // 8 - q // 8).astype(F32)
    gap_z = (p % 8 - q % 8).astype(F32)
    step = (2 * iota((8, 128), 0) + iota((8, 128), 1) // 64 - 7).astype(F32)

    def build(t, carry):
        here = spots[LEAVES + t]
        for n in range(NEARL):
            w = near_leaves[n, t]
            shift = SIDE * (here - spots[w])
            x = step + shift[0:1, :]
            yy, zz = gap_y + shift[1:2, :], gap_z + shift[2:3, :]
            x, flat = x * x, yy * yy + zz * zz + 1.0
            for i in range(8):
                high, low = split(lax.rsqrt(flat + x[i : i + 1, :]))
                tables[t, 128 * n : 128 * n + 64, 128 * i : 128 * i + 128] = high
                tables[t, 128 * n + 64 : 128 * n + 128, 128 * i : 128 * i + 128] = low
        return carry

    lax.fori_loop(0, LEAVES, build, 0)

    for copy in loads[4:]:
        copy.wait()
    arrived(shared_out)
    held = window[...].reshape(32 * HELD, WIDE)
    chosen[...] = jnp.dot(pick_rows[...], held, preferred_element_type=F32).astype(BF16)
    matrix = jnp.dot(chosen[...], pick_columns[...], preferred_element_type=F32)
    local_matrix[0:32, :] = jnp.zeros((32, LEAF), BF16)
    local_matrix[32:, :] = matrix.astype(BF16)

    def window_density(t, carry):
        here = pl.ds(pl.multiple_of(t * LEAF, LEAF), LEAF)
        values = orbitals[here, :]
        product = jnp.dot(values, local_matrix[...], preferred_element_type=F32)
        product = product * values.astype(F32)
        folded[here, :] = (product[:, :128] + product[:, 128:256]) + (
            product[:, 256:384] + product[:, 384:]
        )
        return carry

    lax.fori_loop(0, LEAVES, window_density, 0)

    arrived(hot_c)
    parts = []
    for c in range(5):
        chunk = (me // 4 + 14 + c) % 16
        parts.append(hot_rows[chunk // 2, :, lanes(chunk % 2 * CHUNK, CHUNK)])
    options = [hot_rows[a, :, b * CHUNK : (b + 1) * CHUNK] for a in range(ROW) for b in range(2)]
    parts.append(choose(options, hot // 4))
    matrix = jnp.dot(
        jnp.concatenate(parts, axis=1), pick_columns[...], preferred_element_type=F32
    )
    matrix = jnp.concatenate([matrix, jnp.zeros((96, LEAF), F32)], axis=0).astype(BF16)

    total = jnp.zeros((1, R), F32)
    for t in range(LEAVES):
        here = slice(t * LEAF, (t + 1) * LEAF)
        values = orbitals[here, :]
        product = lax.dot_general(
            values, matrix, (((1,), (1,)), ((), ())), preferred_element_type=F32
        )
        product = product * values[:, :128].astype(F32) + folded[here, :]
        dense = jnp.sum(product.T, axis=0, keepdims=True)
        for i in range(4):
            rho[t * 4 + i : t * 4 + i + 1, :] = dense[:, i * 128 : (i + 1) * 128]
        leaf_moments = jnp.sum(basis[:, here] * dense, axis=1, keepdims=True)
        total = total + jnp.sum(transfer[t] * leaf_moments, axis=0, keepdims=True)
    mine = total
    edge = [
        remote(rho, halo.at[0], e_send.at[0], e_recv.at[0], {"dom": around[2]}),
        remote(rho, halo.at[1], e_send.at[1], e_recv.at[1], {"dom": around[0]}),
    ]
    upward = jnp.sum(dev_transfer[0] * to_column(mine), axis=0, keepdims=True)
    beyond = pltpu.roll(place[...], R, 1)
    mom_mine[0:1, :] = jnp.where(lane < R, jnp.concatenate([mine, mine], axis=1), beyond)
    mom_mine[1:2, :] = jnp.concatenate([upward, upward], axis=1)
    mom_row[j] = mom_mine[...]
    mom_a = send_all(mom_mine, mom_row.at[j], u_send, u_recv, 0, row_peers)
    for copy in edge:
        copy.start()
    rho_store = pltpu.make_async_copy(rho, rho_h, store_sem.at[0])
    rho_store.start()
    zero[...] = jnp.zeros_like(zero)
    zero_store = pltpu.make_async_copy(zero, zero_h, store_sem.at[2])
    zero_store.start()
    arrived(mom_a)
    sums, low, high = jnp.zeros((2, 128), F32), mom_row[0], mom_row[0]
    for b in range(ROW):
        value = mom_row[b]
        bundle[b] = value[0:1]
        sums, low, high = sums + value, jnp.minimum(low, value), jnp.maximum(high, value)
    bounds = jnp.where(lane < R + 3, low[0:1], high[0:1])
    bundle[ROW] = jnp.where(lane < R, sums[1:2], bounds)
    mom_all[y] = bundle[...]
    mom_b = send_all(bundle, mom_all.at[y], u_send, u_recv, 1, column_peers)

    arrived(edge)
    inside = [jnp.where(me > 0, 1.0, 0.0), 1.0, jnp.where(me < N_DOM - 1, 1.0, 0.0)]
    for s, held in enumerate((halo[0], rho[...], halo[1])):
        held = held * inside[s]
        rho_rows[pl.ds(48 * s, 24, stride=2), :] = held[:, :64]
        rho_rows[pl.ds(48 * s + 1, 24, stride=2), :] = held[:, 64:]
    for w in range(3 * LEAVES):
        high, low = split(rho_rows[8 * w : 8 * w + 8, :])
        sources[w] = jnp.concatenate(
            [jnp.concatenate([high, high], axis=1), jnp.concatenate([low, low], axis=1)], axis=0
        )

    def one_near(t, carry):
        lhs = jnp.concatenate([sources[near_leaves[n, t]] for n in range(NEARL)], axis=1)
        both = jnp.dot(lhs, tables[t], preferred_element_type=F32)
        both = both[:8] + both[8:]
        value = jnp.zeros((1, LEAF), F32)
        for qx in range(SIDE):
            value = value + both[qx : qx + 1, (7 - qx) * 64 : (7 - qx) * 64 + LEAF]
        for i in range(4):
            out[pl.ds(4 * t + i, 1), :] = value[:, 128 * i : 128 * i + 128] * vol_weight
        return carry

    lax.fori_loop(0, LEAVES // 2, one_near, 0)

    arrived(mom_b)
    sums, low, high = jnp.zeros((1, 128), F32), mom_all[0, ROW], mom_all[0, ROW]
    for a in range(ROW):
        value = mom_all[a, ROW]
        sums, low, high = sums + value, jnp.minimum(low, value), jnp.maximum(high, value)
    bounds = jnp.where(lane < R + 3, low, high)
    mom_total[...] = jnp.where(lane < R, sums, bounds)
    mom_groups[group] = mom_total[...]
    mom_c = send_all(mom_total, mom_groups.at[group], u_send, u_recv, 2, group_peers)

    far_rows[...] = jnp.zeros_like(far_rows)
    for a in range(ROW):
        for b in range(ROW):
            n = a * ROW + b
            far_rows[n : n + 1, :] = mom_all[a, b]
    mask = jnp.concatenate([dev_far[...], jnp.zeros((1, 128 - N_DOM), jnp.int32)], axis=1)
    flipped = far_rows[...].T
    weights, edges = flipped[:R] * mask.astype(F32), flipped[R : R + 8]
    own, other = [], []
    for d in range(3):
        low, high = SIDE * edges[d : d + 1], SIDE * edges[3 + d : 4 + d] + (SIDE - 1)
        own_low, own_high = first_and_last(coords, d)
        own_low = jnp.full((1, 128), SIDE * own_low).astype(F32)
        own_high = jnp.full((1, 128), SIDE * own_high + (SIDE - 1)).astype(F32)
        own.append((0.5 * (own_low + own_high), 0.5 * (own_high - own_low)))
        other.append((0.5 * (low + high), 0.5 * (high - low)))
    sub = iota((8, 128), 0)
    sites = [[c + h * x for x in CHEB_X] for c, h in own]
    xs = [other[0][0] + other[0][1] * x for x in CHEB_X]
    ys = [other[1][0] + other[1][1] * spread(2 * half + sub // 4, (8, 128)) for half in range(2)]
    zs = other[2][0] + other[2][1] * spread(sub % 4, (8, 128))
    dx = [[(s - x) * (s - x) for x in xs] for s in sites[0]]
    dy = [[(s - v) * (s - v) for v in ys] for s in sites[1]]
    dz = [(s - zs) * (s - zs) + 1.0 for s in sites[2]]
    for b in range(CHEB):
        for e in range(CHEB):
            rest = [v + dz[e] for v in dy[b]]
            for a in range(CHEB):
                running = jnp.zeros((8, 128), F32)
                for t in range(8):
                    value = lax.rsqrt(dx[a][t // 2] + rest[t % 2])
                    running = running + value * weights[8 * t : 8 * t + 8]
                r = a * 16 + b * 4 + e
                partial[8 * r : 8 * r + 8, :] = running
    summed = partial[pl.ds(0, R, stride=8), :]
    for k in range(1, 8):
        summed = summed + partial[pl.ds(k, R, stride=8), :]
    dev_local = jnp.sum(summed, axis=1, keepdims=True)
    node = iota((R, 128), 0)
    point = iota((1, 128), 1) % 64
    own_nodes, far_steps = [], []
    for d, scale in enumerate((16, 4, 1)):
        own_low, own_high = SIDE * bounds[:, R + d : R + d + 1], bounds[:, R + 3 + d : R + 4 + d]
        own_high = SIDE * own_high + (SIDE - 1)
        centre, half = 0.5 * (own_low + own_high), 0.5 * (own_high - own_low)
        own_nodes.append(centre + half * spread(node // scale % 4, (R, 128)))
        far_steps.append(spread(point // scale % 4, (1, 128)))

    lax.fori_loop(LEAVES // 2, LEAVES, one_near, 0)

    arrived(mom_c)
    left = lane < R
    summed = jnp.zeros((R, 128), F32)
    for i in range(N_GROUP // 2):
        one, two = mom_groups[2 * i], mom_groups[2 * i + 1]
        square = jnp.full((R, 128), 1.0, F32)
        for d in range(3):
            at, to = slice(R + d, R + d + 1), slice(R + 3 + d, R + 4 + d)
            low = SIDE * jnp.where(left, one[:, at], two[:, at])
            high = jnp.where(left, one[:, to], two[:, to])
            high = SIDE * high + (SIDE - 1)
            gap = own_nodes[d] - (0.5 * (low + high) + 0.5 * (high - low) * far_steps[d])
            square = square + gap * gap
        mask = jnp.where(left, group_far[0, 2 * i], group_far[0, 2 * i + 1]).astype(F32)
        weight = jnp.concatenate([one[:, :R], two[:, :R]], axis=1) * mask
        summed = summed + lax.rsqrt(square) * weight
    group_local = to_row(jnp.sum(summed, axis=1, keepdims=True))
    dev_total = dev_local + jnp.sum(dev_transfer[0] * group_local, axis=1, keepdims=True)
    dev_total = to_row(dev_total * vol_weight)
    for t in range(LEAVES):
        leaf_local = jnp.sum(transfer[t] * dev_total, axis=1, keepdims=True)
        far = jnp.sum(basis[:, t * LEAF : (t + 1) * LEAF] * leaf_local, axis=0, keepdims=True)
        for i in range(4):
            out[4 * t + i : 4 * t + i + 1, :] += far[:, 128 * i : 128 * i + 128]
    out_store = pltpu.make_async_copy(out, out_h, store_sem.at[1])
    out_store.start()
    for copy in hot_a + hot_b + hot_c + wide + shared_out + beside + mom_a + mom_b + mom_c + edge:
        copy.wait_send()
    rho_store.wait()
    zero_store.wait()
    out_store.wait()


def local(
    orbitals, density_rows, near_blocks, leaf_coords, near_leaves, leaf_basis, leaf_transfer,
    dev_transfer, dev_far, group_far,
):
    anywhere = pl.BlockSpec(memory_space=pl.ANY)
    rows = pltpu.VMEM((1, 128), F32)
    slab = pltpu.VMEM((4 * LEAVES, 128), F32)
    sems = pltpu.SemaphoreType.DMA
    density, hartree, zero = pl.pallas_call(
        kernel,
        out_shape=(jax.ShapeDtypeStruct((4 * LEAVES, 128), F32),) * 3,
        in_specs=[anywhere] * 10,
        out_specs=(anywhere,) * 3,
        scratch_shapes=[
            pltpu.SMEM((1, NEAR_B), jnp.int32),
            pltpu.SMEM((3, LEAVES), jnp.int32),
            pltpu.SMEM((NEARL, LEAVES), jnp.int32),
            pltpu.SMEM((1, N_GROUP), jnp.int32),
            pltpu.VMEM((1, N_DOM), jnp.int32),
            pltpu.VMEM((LEAVES * LEAF, LEAF), BF16),
            pltpu.VMEM((32, 16 * CHUNK), BF16),
            pltpu.VMEM((R, LEAVES * LEAF), F32),
            pltpu.VMEM((LEAVES, R, R), F32),
            pltpu.VMEM((1, R, R), F32),
            slab, slab, slab,
            pltpu.VMEM((5, 32, WIDE), BF16),
            pltpu.VMEM((HELD, 32, WIDE), BF16),
            pltpu.VMEM((ROW, 32, 256), BF16),
            pltpu.VMEM((32, 256), BF16),
            pltpu.VMEM((ROW, 32, 256), BF16),
            pltpu.VMEM((32, 256), BF16),
            pltpu.VMEM((ROW, 32, 256), BF16),
            rows,
            pltpu.VMEM((3, 1, 128), F32),
            pltpu.VMEM((2, 128), F32),
            pltpu.VMEM((ROW, 2, 128), F32),
            pltpu.VMEM((ROW + 1, 1, 128), F32),
            pltpu.VMEM((ROW, ROW + 1, 1, 128), F32),
            rows,
            pltpu.VMEM((N_GROUP, 1, 128), F32),
            pltpu.VMEM((2, 4 * LEAVES, 128), F32),
            pltpu.VMEM((LEAF - 32, 32 * HELD), BF16),
            pltpu.VMEM((WIDE, LEAF), BF16),
            pltpu.VMEM((LEAF - 32, WIDE), BF16),
            pltpu.VMEM((LEAF, LEAF), BF16),
            pltpu.VMEM((LEAVES * LEAF, 128), F32),
            pltpu.VMEM((24 * LEAVES, 64), F32),
            pltpu.VMEM((3 * LEAVES, 16, 128), BF16),
            pltpu.VMEM((3 * LEAVES, 8, 128), F32),
            pltpu.VMEM((LEAVES, 128 * NEARL, 1024), BF16),
            pltpu.VMEM((128, 128), F32),
            pltpu.VMEM((8 * R, 128), F32),
            sems((10,)), sems((3,)),
            sems((2, 9)), sems((2, 9)),
            sems((3, ROW - 1)), sems((3, ROW - 1)),
            sems((3, ROW - 1)), sems((3, ROW - 1)),
            sems((4,)), sems((4,)),
        ],
        compiler_params=pltpu.CompilerParams(
            collective_id=0, has_side_effects=True, vmem_limit_bytes=60 << 20
        ),
    )(
        near_blocks, leaf_coords, near_leaves.T, group_far, dev_far, orbitals, density_rows,
        leaf_basis, leaf_transfer, dev_transfer,
    )
    return ((density + zero).reshape(-1), (hartree + zero).reshape(-1))


def solution(mesh):
    in_specs = (
        P(("group", "dom"), None),
        P(("group", "dom"), None),
        P(("group", "dom"), None),
        P(None, ("group", "dom")),
        P(("group", "dom"), None),
        P(None, ("group", "dom")),
        P(("group", "dom"), None, None),
        P(("group", "dom"), None, None),
        P(("group", "dom"), None),
        P("group", None),
    )
    out_specs = (P(("group", "dom")), P(("group", "dom")))
    return jax.shard_map(local, mesh=mesh, in_specs=in_specs, out_specs=out_specs, check_vma=False)
```

```python
import functools
import math

import jax
import jax.numpy as jnp
from jax import lax
from jax.experimental import pallas as pl
from jax.experimental.pallas import tpu as pltpu
from jax.sharding import PartitionSpec as P

SIDE = 8
LEAF = 512
CHEB = 4
R = 64
BW = 16
NEAR_B = 32
REACH = 8
LEAVES = 6
NEARL = 3
N_DOM = 64
N_GROUP = 8
ROW = 8
FAR_FIRST = (4, 3, 5, 2, 6, 1, 7)
CHUNK = 128
SPAN = REACH // 2
HELD = 2 * (2 * SPAN + 1)
WIDE = 6 * CHUNK

vol_weight = 0.1
MESH = pl.DeviceIdType.MESH
F32 = jnp.float32
BF16 = jnp.bfloat16
CHEB_X = [math.cos((2 * a + 1) * math.pi / (2 * CHEB)) for a in range(CHEB)]


def lanes(start, size):
    return pl.ds(pl.multiple_of(start, size), size)


def remote(src, dst, send, recv, device):
    return pltpu.make_async_remote_copy(
        src_ref=src, dst_ref=dst, send_sem=send, recv_sem=recv, device_id=device, device_id_type=MESH
    )


def signal(barrier, device):
    pl.semaphore_signal(barrier, inc=1, device_id=device, device_id_type=MESH)


def choose(pieces, index):
    piece = pieces[0]
    for s in range(1, len(pieces)):
        piece = jnp.where(index == s, pieces[s], piece)
    return piece


def eye64():
    return lax.broadcasted_iota(jnp.int32, (R, R), 0) == lax.broadcasted_iota(jnp.int32, (R, R), 1)


def to_column(row):
    return jnp.sum(jnp.where(eye64(), row, 0.0), axis=1, keepdims=True)


def to_row(column):
    return jnp.sum(jnp.where(eye64(), column, 0.0), axis=0, keepdims=True)


def split(value):
    high = value.astype(BF16)
    return high, (value - high.astype(F32)).astype(BF16)


def iota(shape, dim):
    return lax.broadcasted_iota(jnp.int32, shape, dim)


def first_and_last(coords, d):
    first = last = coords[d, 0]
    for t in range(1, LEAVES):
        first = jnp.minimum(first, coords[d, t])
        last = jnp.maximum(last, coords[d, t])
    return first, last


def spread(index, shape):
    value = jnp.full(shape, CHEB_X[0], F32)
    for a in range(1, CHEB):
        value = jnp.where(index == a, CHEB_X[a], value)
    return value


def kernel(
    near_h, coords_h, near_leaves_h, group_far_h, dev_far_h,
    orbitals_h, rows_h, basis_h, transfer_h, dev_transfer_h,
    rho_h, out_h, zero_h,
    near, coords, near_leaves, group_far, dev_far,
    orbitals, rows, basis, transfer, dev_transfer, rho, out, zero,
    stage, window, first, passed, second, kept, hot_rows,
    place, places, mom_mine, mom_row, bundle, mom_all, mom_total, mom_groups,
    halo, pick_rows, pick_columns, chosen, local_matrix, folded,
    rho_rows, sources, spots, tables, far_rows, partial,
    load_sem, store_sem, w_send, w_recv, h_send, h_recv, u_send, u_recv, e_send, e_recv,
):
    me = lax.axis_index("dom")
    group = lax.axis_index("group")
    y, j = me // ROW, me % ROW
    core, chip = me % 2, me // 2
    chips = [s * o for o in range(SPAN, 0, -1) for s in (1, -1)]
    sibling = {"dom": me + 1 - 2 * core}
    row_peers = [{"dom": y * ROW + (j + d) % ROW} for d in FAR_FIRST]
    column_peers = [{"dom": (me + d * ROW) % N_DOM} for d in FAR_FIRST]
    group_peers = [{"group": (group + d) % N_GROUP} for d in FAR_FIRST]
    window_peers = [{"dom": (me + 2 * o + N_DOM) % N_DOM} for o in chips]
    around = [(me + N_DOM - 1) % N_DOM, me, (me + 1) % N_DOM]
    peers = window_peers + row_peers + [{"dom": around[0]}, {"dom": around[2]}]
    peers = peers + [p for d, p in zip(FAR_FIRST, column_peers) if 1 < d < ROW - 1] + group_peers
    barrier = pltpu.get_barrier_semaphore()
    for peer in peers:
        signal(barrier, peer)
    loads = []
    for n, (src, dst) in enumerate(
        (
            (rows_h, rows),
            (near_h, near),
            (coords_h, coords),
            (near_leaves_h, near_leaves),
            (group_far_h, group_far),
            (dev_far_h, dev_far),
            (orbitals_h, orbitals),
            (basis_h, basis),
            (transfer_h, transfer),
            (dev_transfer_h, dev_transfer),
        )
    ):
        loads.append(pltpu.make_async_copy(src, dst, load_sem.at[n]))
    for copy in loads[:6]:
        copy.start()

    def send_all(src, dst, sends, recvs, phase, targets):
        copies = []
        for d, peer in enumerate(targets):
            copy = remote(src, dst, sends.at[phase, d], recvs.at[phase, d], peer)
            copy.start()
            copies.append(copy)
        return copies

    def arrived(copies):
        for copy in copies:
            copy.wait_recv()

    loads[0].wait()
    loads[1].wait()
    hot = near[0, 0] // 2
    base = (me + N_DOM - REACH) // 4
    shared = choose([rows[:, c * CHUNK : (c + 1) * CHUNK] for c in range(16)], hot // 4)
    for kk in range(5):
        for c in range(5):
            chunk = (base + kk + c - 2) % 16
            stage[kk, :, c * CHUNK : (c + 1) * CHUNK] = rows[:, lanes(chunk * CHUNK, CHUNK)]
        stage[kk, :, 5 * CHUNK :] = shared
    window[2 * SPAN + core] = stage[2]
    first[j] = rows[:, lanes(j * 256, 256)]
    loads[2].wait()
    lane = iota((1, 128), 1)
    packed = jnp.zeros((1, 128), jnp.int32)
    for d in range(3):
        low, high = first_and_last(coords, d)
        packed = jnp.where(lane == d, low, packed)
        packed = jnp.where(lane == 3 + d, high, packed)
        for t in range(LEAVES):
            packed = jnp.where(lane == 8 + 3 * t + d, coords[d, t], packed)
    place[...] = packed.astype(F32)
    places[1] = place[...]
    pl.semaphore_wait(barrier, len(peers))

    hot_a = []
    for n, d in enumerate(FAR_FIRST):
        to = (j + d) % ROW
        copy = remote(
            rows.at[:, lanes(to * 256, 256)], first.at[j], h_send.at[0, n], h_recv.at[0, n], row_peers[n]
        )
        copy.start()
        hot_a.append(copy)
    wide = []
    for n, o in enumerate(chips):
        kk = (me + 2 * o + N_DOM) // 4 - base
        slot = 2 * (SPAN - o) + core
        copy = remote(stage.at[kk], window.at[slot], w_send.at[0, n], w_recv.at[0, n], window_peers[n])
        copy.start()
        wide.append(copy)
    own = window.at[2 * SPAN + core]
    shared_out = [remote(own, own, w_send.at[1, 8], w_recv.at[1, 8], sibling)]
    shared_out[0].start()
    beside = [
        remote(place, places.at[0], e_send.at[2], e_recv.at[2], {"dom": around[2]}),
        remote(place, places.at[2], e_send.at[3], e_recv.at[3], {"dom": around[0]}),
    ]
    for copy in beside + loads[6:]:
        copy.start()

    arrived(hot_a)
    piece = choose([first[s] for s in range(ROW)], hot % ROW)
    passed[...] = piece
    second[y] = piece
    hot_b = send_all(passed, second.at[y], h_send, h_recv, 1, column_peers)
    gap = iota((BW, 640), 1) - iota((BW, 640), 0)
    for k in range(2, NEAR_B):
        block = near[0, k]
        slot = (block // 4 - chip + SPAN + N_DOM // 2) % (N_DOM // 2) * 2 + block // 2 % 2
        start = slot * 32 + block % 2 * BW
        part = jnp.where(gap == start, 1.0, 0.0)[:, : 32 * HELD]
        pick_rows[(k - 2) * BW : (k - 1) * BW, :] = part.astype(BF16)
    wide_lane = iota((1, LEAF), 1)
    start = jnp.zeros((1, LEAF), jnp.int32)
    for k in range(NEAR_B):
        block = near[0, k]
        chunk = 5 if k < 2 else (block // 8 - me // 4 + 18) % 16
        start = jnp.where(wide_lane // BW == k, chunk * CHUNK + block % 8 * BW, start)
    start = start + wide_lane % BW
    pick = jnp.where(iota((WIDE, LEAF), 0) == start, 1.0, 0.0)
    pick_columns[...] = pick.astype(BF16)

    for n, o in enumerate(chips):
        wide[n].wait_recv()
        piece = window.at[2 * (SPAN - o) + core]
        copy = remote(piece, piece, w_send.at[1, n], w_recv.at[1, n], sibling)
        copy.start()
        shared_out.append(copy)
    arrived(hot_b)
    piece = choose([second[s] for s in range(ROW)], hot // ROW)
    kept[...] = piece
    hot_rows[j] = piece
    hot_c = send_all(kept, hot_rows.at[j], h_send, h_recv, 2, row_peers)
    for copy in loads[4:]:
        copy.wait()
    arrived(shared_out)
    held = window[...].reshape(32 * HELD, WIDE)
    chosen[...] = jnp.dot(pick_rows[...], held, preferred_element_type=F32).astype(BF16)
    matrix = jnp.dot(chosen[...], pick_columns[...], preferred_element_type=F32)
    local_matrix[0:32, :] = jnp.zeros((32, LEAF), BF16)
    local_matrix[32:, :] = matrix.astype(BF16)

    def window_density(t, carry):
        here = pl.ds(pl.multiple_of(t * LEAF, LEAF), LEAF)
        values = orbitals[here, :]
        product = jnp.dot(values, local_matrix[...], preferred_element_type=F32)
        product = product * values.astype(F32)
        folded[here, :] = (product[:, :128] + product[:, 128:256]) + (
            product[:, 256:384] + product[:, 384:]
        )
        return carry

    lax.fori_loop(0, LEAVES, window_density, 0)

    arrived(hot_c)
    parts = []
    for c in range(5):
        chunk = (me // 4 + 14 + c) % 16
        parts.append(hot_rows[chunk // 2, :, lanes(chunk % 2 * CHUNK, CHUNK)])
    options = [hot_rows[a, :, b * CHUNK : (b + 1) * CHUNK] for a in range(ROW) for b in range(2)]
    parts.append(choose(options, hot // 4))
    matrix = jnp.dot(
        jnp.concatenate(parts, axis=1), pick_columns[...], preferred_element_type=F32
    )
    matrix = jnp.concatenate([matrix, jnp.zeros((96, LEAF), F32)], axis=0).astype(BF16)

    total = jnp.zeros((1, R), F32)
    for t in range(LEAVES):
        here = slice(t * LEAF, (t + 1) * LEAF)
        values = orbitals[here, :]
        product = lax.dot_general(
            values, matrix, (((1,), (1,)), ((), ())), preferred_element_type=F32
        )
        product = product * values[:, :128].astype(F32) + folded[here, :]
        dense = jnp.sum(product.T, axis=0, keepdims=True)
        for i in range(4):
            rho[t * 4 + i : t * 4 + i + 1, :] = dense[:, i * 128 : (i + 1) * 128]
        leaf_moments = jnp.sum(basis[:, here] * dense, axis=1, keepdims=True)
        total = total + jnp.sum(transfer[t] * leaf_moments, axis=0, keepdims=True)
    mine = total
    edge = [
        remote(rho, halo.at[0], e_send.at[0], e_recv.at[0], {"dom": around[2]}),
        remote(rho, halo.at[1], e_send.at[1], e_recv.at[1], {"dom": around[0]}),
    ]
    upward = jnp.sum(dev_transfer[0] * to_column(mine), axis=0, keepdims=True)
    beyond = pltpu.roll(place[...], R, 1)
    mom_mine[0:1, :] = jnp.where(lane < R, jnp.concatenate([mine, mine], axis=1), beyond)
    mom_mine[1:2, :] = jnp.concatenate([upward, upward], axis=1)
    mom_row[j] = mom_mine[...]
    mom_a = send_all(mom_mine, mom_row.at[j], u_send, u_recv, 0, row_peers)
    for copy in edge:
        copy.start()
    rho_store = pltpu.make_async_copy(rho, rho_h, store_sem.at[0])
    rho_store.start()
    zero[...] = jnp.zeros_like(zero)
    zero_store = pltpu.make_async_copy(zero, zero_h, store_sem.at[2])
    zero_store.start()

    loads[3].wait()
    arrived(beside)
    for s in range(3):
        held = places[s]
        for t in range(LEAVES):
            for d in range(3):
                k = 8 + 3 * t + d
                spots[s * LEAVES + t, d : d + 1, :] = jnp.broadcast_to(held[:, k : k + 1], (1, 128))
    q = iota((64, 128), 0)
    p = iota((64, 128), 1) % 64
    gap_y = (p // 8 - q // 8).astype(F32)
    gap_z = (p % 8 - q % 8).astype(F32)
    step = (2 * iota((8, 128), 0) + iota((8, 128), 1) // 64 - 7).astype(F32)

    def build(t, carry):
        here = spots[LEAVES + t]
        for n in range(NEARL):
            w = near_leaves[n, t]
            shift = SIDE * (here - spots[w])
            x = step + shift[0:1, :]
            yy, zz = gap_y + shift[1:2, :], gap_z + shift[2:3, :]
            x, flat = x * x, yy * yy + zz * zz + 1.0
            for i in range(8):
                high, low = split(lax.rsqrt(flat + x[i : i + 1, :]))
                tables[t, 128 * n : 128 * n + 64, 128 * i : 128 * i + 128] = high
                tables[t, 128 * n + 64 : 128 * n + 128, 128 * i : 128 * i + 128] = low
        return carry

    lax.fori_loop(0, LEAVES, build, 0)

    arrived(mom_a)
    sums, low, high = jnp.zeros((2, 128), F32), mom_row[0], mom_row[0]
    for b in range(ROW):
        value = mom_row[b]
        bundle[b] = value[0:1]
        sums, low, high = sums + value, jnp.minimum(low, value), jnp.maximum(high, value)
    bounds = jnp.where(lane < R + 3, low[0:1], high[0:1])
    bundle[ROW] = jnp.where(lane < R, sums[1:2], bounds)
    mom_all[y] = bundle[...]
    mom_b = send_all(bundle, mom_all.at[y], u_send, u_recv, 1, column_peers)

    arrived(edge)
    inside = [jnp.where(me > 0, 1.0, 0.0), 1.0, jnp.where(me < N_DOM - 1, 1.0, 0.0)]
    for s, held in enumerate((halo[0], rho[...], halo[1])):
        held = held * inside[s]
        rho_rows[pl.ds(48 * s, 24, stride=2), :] = held[:, :64]
        rho_rows[pl.ds(48 * s + 1, 24, stride=2), :] = held[:, 64:]
    for w in range(3 * LEAVES):
        high, low = split(rho_rows[8 * w : 8 * w + 8, :])
        sources[w] = jnp.concatenate(
            [jnp.concatenate([high, high], axis=1), jnp.concatenate([low, low], axis=1)], axis=0
        )

    def one_near(t, carry):
        lhs = jnp.concatenate([sources[near_leaves[n, t]] for n in range(NEARL)], axis=1)
        both = jnp.dot(lhs, tables[t], preferred_element_type=F32)
        both = both[:8] + both[8:]
        value = jnp.zeros((1, LEAF), F32)
        for qx in range(SIDE):
            value = value + both[qx : qx + 1, (7 - qx) * 64 : (7 - qx) * 64 + LEAF]
        for i in range(4):
            out[pl.ds(4 * t + i, 1), :] = value[:, 128 * i : 128 * i + 128] * vol_weight
        return carry

    lax.fori_loop(0, LEAVES // 2, one_near, 0)

    arrived(mom_b)
    sums, low, high = jnp.zeros((1, 128), F32), mom_all[0, ROW], mom_all[0, ROW]
    for a in range(ROW):
        value = mom_all[a, ROW]
        sums, low, high = sums + value, jnp.minimum(low, value), jnp.maximum(high, value)
    bounds = jnp.where(lane < R + 3, low, high)
    mom_total[...] = jnp.where(lane < R, sums, bounds)
    mom_groups[group] = mom_total[...]
    mom_c = send_all(mom_total, mom_groups.at[group], u_send, u_recv, 2, group_peers)

    far_rows[...] = jnp.zeros_like(far_rows)
    for a in range(ROW):
        for b in range(ROW):
            n = a * ROW + b
            far_rows[n : n + 1, :] = mom_all[a, b]
    mask = jnp.concatenate([dev_far[...], jnp.zeros((1, 128 - N_DOM), jnp.int32)], axis=1)
    flipped = far_rows[...].T
    weights, edges = flipped[:R] * mask.astype(F32), flipped[R : R + 8]
    own, other = [], []
    for d in range(3):
        low, high = SIDE * edges[d : d + 1], SIDE * edges[3 + d : 4 + d] + (SIDE - 1)
        own_low, own_high = first_and_last(coords, d)
        own_low = jnp.full((1, 128), SIDE * own_low).astype(F32)
        own_high = jnp.full((1, 128), SIDE * own_high + (SIDE - 1)).astype(F32)
        own.append((0.5 * (own_low + own_high), 0.5 * (own_high - own_low)))
        other.append((0.5 * (low + high), 0.5 * (high - low)))
    sub = iota((8, 128), 0)
    sites = [[c + h * x for x in CHEB_X] for c, h in own]
    xs = [other[0][0] + other[0][1] * x for x in CHEB_X]
    ys = [other[1][0] + other[1][1] * spread(2 * half + sub // 4, (8, 128)) for half in range(2)]
    zs = other[2][0] + other[2][1] * spread(sub % 4, (8, 128))
    dx = [[(s - x) * (s - x) for x in xs] for s in sites[0]]
    dy = [[(s - v) * (s - v) for v in ys] for s in sites[1]]
    dz = [(s - zs) * (s - zs) + 1.0 for s in sites[2]]
    for b in range(CHEB):
        for e in range(CHEB):
            rest = [v + dz[e] for v in dy[b]]
            for a in range(CHEB):
                running = jnp.zeros((8, 128), F32)
                for t in range(8):
                    value = lax.rsqrt(dx[a][t // 2] + rest[t % 2])
                    running = running + value * weights[8 * t : 8 * t + 8]
                r = a * 16 + b * 4 + e
                partial[8 * r : 8 * r + 8, :] = running
    summed = partial[pl.ds(0, R, stride=8), :]
    for k in range(1, 8):
        summed = summed + partial[pl.ds(k, R, stride=8), :]
    dev_local = jnp.sum(summed, axis=1, keepdims=True)
    node = iota((R, 128), 0)
    point = iota((1, 128), 1) % 64
    own_nodes, far_steps = [], []
    for d, scale in enumerate((16, 4, 1)):
        own_low, own_high = SIDE * bounds[:, R + d : R + d + 1], bounds[:, R + 3 + d : R + 4 + d]
        own_high = SIDE * own_high + (SIDE - 1)
        centre, half = 0.5 * (own_low + own_high), 0.5 * (own_high - own_low)
        own_nodes.append(centre + half * spread(node // scale % 4, (R, 128)))
        far_steps.append(spread(point // scale % 4, (1, 128)))

    lax.fori_loop(LEAVES // 2, LEAVES, one_near, 0)

    arrived(mom_c)
    left = lane < R
    summed = jnp.zeros((R, 128), F32)
    for i in range(N_GROUP // 2):
        one, two = mom_groups[2 * i], mom_groups[2 * i + 1]
        square = jnp.full((R, 128), 1.0, F32)
        for d in range(3):
            at, to = slice(R + d, R + d + 1), slice(R + 3 + d, R + 4 + d)
            low = SIDE * jnp.where(left, one[:, at], two[:, at])
            high = jnp.where(left, one[:, to], two[:, to])
            high = SIDE * high + (SIDE - 1)
            gap = own_nodes[d] - (0.5 * (low + high) + 0.5 * (high - low) * far_steps[d])
            square = square + gap * gap
        mask = jnp.where(left, group_far[0, 2 * i], group_far[0, 2 * i + 1]).astype(F32)
        weight = jnp.concatenate([one[:, :R], two[:, :R]], axis=1) * mask
        summed = summed + lax.rsqrt(square) * weight
    group_local = to_row(jnp.sum(summed, axis=1, keepdims=True))
    dev_total = dev_local + jnp.sum(dev_transfer[0] * group_local, axis=1, keepdims=True)
    dev_total = to_row(dev_total * vol_weight)
    for t in range(LEAVES):
        leaf_local = jnp.sum(transfer[t] * dev_total, axis=1, keepdims=True)
        far = jnp.sum(basis[:, t * LEAF : (t + 1) * LEAF] * leaf_local, axis=0, keepdims=True)
        for i in range(4):
            out[4 * t + i : 4 * t + i + 1, :] += far[:, 128 * i : 128 * i + 128]
    out_store = pltpu.make_async_copy(out, out_h, store_sem.at[1])
    out_store.start()
    for copy in hot_a + hot_b + hot_c + wide + shared_out + beside + mom_a + mom_b + mom_c + edge:
        copy.wait_send()
    rho_store.wait()
    zero_store.wait()
    out_store.wait()


def local(
    orbitals, density_rows, near_blocks, leaf_coords, near_leaves, leaf_basis, leaf_transfer,
    dev_transfer, dev_far, group_far,
):
    anywhere = pl.BlockSpec(memory_space=pl.ANY)
    rows = pltpu.VMEM((1, 128), F32)
    slab = pltpu.VMEM((4 * LEAVES, 128), F32)
    sems = pltpu.SemaphoreType.DMA
    density, hartree, zero = pl.pallas_call(
        kernel,
        out_shape=(jax.ShapeDtypeStruct((4 * LEAVES, 128), F32),) * 3,
        in_specs=[anywhere] * 10,
        out_specs=(anywhere,) * 3,
        scratch_shapes=[
            pltpu.SMEM((1, NEAR_B), jnp.int32),
            pltpu.SMEM((3, LEAVES), jnp.int32),
            pltpu.SMEM((NEARL, LEAVES), jnp.int32),
            pltpu.SMEM((1, N_GROUP), jnp.int32),
            pltpu.VMEM((1, N_DOM), jnp.int32),
            pltpu.VMEM((LEAVES * LEAF, LEAF), BF16),
            pltpu.VMEM((32, 16 * CHUNK), BF16),
            pltpu.VMEM((R, LEAVES * LEAF), F32),
            pltpu.VMEM((LEAVES, R, R), F32),
            pltpu.VMEM((1, R, R), F32),
            slab, slab, slab,
            pltpu.VMEM((5, 32, WIDE), BF16),
            pltpu.VMEM((HELD, 32, WIDE), BF16),
            pltpu.VMEM((ROW, 32, 256), BF16),
            pltpu.VMEM((32, 256), BF16),
            pltpu.VMEM((ROW, 32, 256), BF16),
            pltpu.VMEM((32, 256), BF16),
            pltpu.VMEM((ROW, 32, 256), BF16),
            rows,
            pltpu.VMEM((3, 1, 128), F32),
            pltpu.VMEM((2, 128), F32),
            pltpu.VMEM((ROW, 2, 128), F32),
            pltpu.VMEM((ROW + 1, 1, 128), F32),
            pltpu.VMEM((ROW, ROW + 1, 1, 128), F32),
            rows,
            pltpu.VMEM((N_GROUP, 1, 128), F32),
            pltpu.VMEM((2, 4 * LEAVES, 128), F32),
            pltpu.VMEM((LEAF - 32, 32 * HELD), BF16),
            pltpu.VMEM((WIDE, LEAF), BF16),
            pltpu.VMEM((LEAF - 32, WIDE), BF16),
            pltpu.VMEM((LEAF, LEAF), BF16),
            pltpu.VMEM((LEAVES * LEAF, 128), F32),
            pltpu.VMEM((24 * LEAVES, 64), F32),
            pltpu.VMEM((3 * LEAVES, 16, 128), BF16),
            pltpu.VMEM((3 * LEAVES, 8, 128), F32),
            pltpu.VMEM((LEAVES, 128 * NEARL, 1024), BF16),
            pltpu.VMEM((128, 128), F32),
            pltpu.VMEM((8 * R, 128), F32),
            sems((10,)), sems((3,)),
            sems((2, 9)), sems((2, 9)),
            sems((3, ROW - 1)), sems((3, ROW - 1)),
            sems((3, ROW - 1)), sems((3, ROW - 1)),
            sems((4,)), sems((4,)),
        ],
        compiler_params=pltpu.CompilerParams(
            collective_id=0, has_side_effects=True, vmem_limit_bytes=60 << 20
        ),
    )(
        near_blocks, leaf_coords, near_leaves.T, group_far, dev_far, orbitals, density_rows,
        leaf_basis, leaf_transfer, dev_transfer,
    )
    return ((density + zero).reshape(-1), (hartree + zero).reshape(-1))


def solution(mesh):
    in_specs = (
        P(("group", "dom"), None),
        P(("group", "dom"), None),
        P(("group", "dom"), None),
        P(None, ("group", "dom")),
        P(("group", "dom"), None),
        P(None, ("group", "dom")),
        P(("group", "dom"), None, None),
        P(("group", "dom"), None, None),
        P(("group", "dom"), None),
        P("group", None),
    )
    out_specs = (P(("group", "dom")), P(("group", "dom")))
    return jax.shard_map(local, mesh=mesh, in_specs=in_specs, out_specs=out_specs, check_vma=False)
```

```python
import functools
import math

import jax
import jax.numpy as jnp
from jax import lax
from jax.experimental import pallas as pl
from jax.experimental.pallas import tpu as pltpu
from jax.sharding import PartitionSpec as P

SIDE = 8
LEAF = 512
CHEB = 4
R = 64
BW = 16
NEAR_B = 32
REACH = 8
LEAVES = 6
NEARL = 3
N_DOM = 64
N_GROUP = 8
ROW = 8
FAR_FIRST = (4, 3, 5, 2, 6, 1, 7)
CHUNK = 128
SPAN = REACH // 2
HELD = 2 * (2 * SPAN + 1)
WIDE = 6 * CHUNK

vol_weight = 0.1
MESH = pl.DeviceIdType.MESH
F32 = jnp.float32
BF16 = jnp.bfloat16
CHEB_X = [math.cos((2 * a + 1) * math.pi / (2 * CHEB)) for a in range(CHEB)]


def lanes(start, size):
    return pl.ds(pl.multiple_of(start, size), size)


def remote(src, dst, send, recv, device):
    return pltpu.make_async_remote_copy(
        src_ref=src, dst_ref=dst, send_sem=send, recv_sem=recv, device_id=device, device_id_type=MESH
    )


def signal(barrier, device):
    pl.semaphore_signal(barrier, inc=1, device_id=device, device_id_type=MESH)


def choose(pieces, index):
    piece = pieces[0]
    for s in range(1, len(pieces)):
        piece = jnp.where(index == s, pieces[s], piece)
    return piece


def eye64():
    return lax.broadcasted_iota(jnp.int32, (R, R), 0) == lax.broadcasted_iota(jnp.int32, (R, R), 1)


def to_column(row):
    return jnp.sum(jnp.where(eye64(), row, 0.0), axis=1, keepdims=True)


def to_row(column):
    return jnp.sum(jnp.where(eye64(), column, 0.0), axis=0, keepdims=True)


def split(value):
    high = value.astype(BF16)
    return high, (value - high.astype(F32)).astype(BF16)


def iota(shape, dim):
    return lax.broadcasted_iota(jnp.int32, shape, dim)


def first_and_last(coords, d):
    first = last = coords[d, 0]
    for t in range(1, LEAVES):
        first = jnp.minimum(first, coords[d, t])
        last = jnp.maximum(last, coords[d, t])
    return first, last


def spread(index, shape):
    value = jnp.full(shape, CHEB_X[0], F32)
    for a in range(1, CHEB):
        value = jnp.where(index == a, CHEB_X[a], value)
    return value


def kernel(
    near_h, coords_h, near_leaves_h, group_far_h, dev_far_h,
    orbitals_h, rows_h, basis_h, transfer_h, dev_transfer_h,
    rho_h, out_h, zero_h,
    near, coords, near_leaves, group_far, dev_far,
    orbitals, rows, basis, transfer, dev_transfer, rho, out, zero,
    stage, window, first, passed, second, kept, hot_rows,
    place, places, mom_mine, mom_row, bundle, mom_all, mom_total, mom_groups,
    halo, pick_rows, pick_columns, chosen, local_matrix, folded,
    rho_rows, sources, spots, tables, far_rows, partial,
    load_sem, store_sem, w_send, w_recv, h_send, h_recv, u_send, u_recv, e_send, e_recv,
):
    me = lax.axis_index("dom")
    group = lax.axis_index("group")
    y, j = me // ROW, me % ROW
    core, chip = me % 2, me // 2
    chips = [s * o for o in range(SPAN, 0, -1) for s in (1, -1)]
    sibling = {"dom": me + 1 - 2 * core}
    row_peers = [{"dom": y * ROW + (j + d) % ROW} for d in FAR_FIRST]
    column_peers = [{"dom": (me + d * ROW) % N_DOM} for d in FAR_FIRST]
    group_peers = [{"group": (group + d) % N_GROUP} for d in FAR_FIRST]
    window_peers = [{"dom": (me + 2 * o + N_DOM) % N_DOM} for o in chips]
    around = [(me + N_DOM - 1) % N_DOM, me, (me + 1) % N_DOM]
    peers = window_peers + row_peers + [{"dom": around[0]}, {"dom": around[2]}]
    peers = peers + [p for d, p in zip(FAR_FIRST, column_peers) if 1 < d < ROW - 1] + group_peers
    barrier = pltpu.get_barrier_semaphore()
    for peer in peers:
        signal(barrier, peer)
    loads = []
    for n, (src, dst) in enumerate(
        (
            (rows_h, rows),
            (near_h, near),
            (coords_h, coords),
            (near_leaves_h, near_leaves),
            (group_far_h, group_far),
            (dev_far_h, dev_far),
            (orbitals_h, orbitals),
            (basis_h, basis),
            (transfer_h, transfer),
            (dev_transfer_h, dev_transfer),
        )
    ):
        loads.append(pltpu.make_async_copy(src, dst, load_sem.at[n]))
    for copy in loads[:6]:
        copy.start()

    def send_all(src, dst, sends, recvs, phase, targets):
        copies = []
        for d, peer in enumerate(targets):
            copy = remote(src, dst, sends.at[phase, d], recvs.at[phase, d], peer)
            copy.start()
            copies.append(copy)
        return copies

    def arrived(copies):
        for copy in copies:
            copy.wait_recv()

    loads[0].wait()
    loads[1].wait()
    hot = near[0, 0] // 2
    base = (me + N_DOM - REACH) // 4
    shared = choose([rows[:, c * CHUNK : (c + 1) * CHUNK] for c in range(16)], hot // 4)
    for kk in range(5):
        for c in range(5):
            chunk = (base + kk + c - 2) % 16
            stage[kk, :, c * CHUNK : (c + 1) * CHUNK] = rows[:, lanes(chunk * CHUNK, CHUNK)]
        stage[kk, :, 5 * CHUNK :] = shared
    window[2 * SPAN + core] = stage[2]
    first[j] = rows[:, lanes(j * 256, 256)]
    loads[2].wait()
    lane = iota((1, 128), 1)
    packed = jnp.zeros((1, 128), jnp.int32)
    for d in range(3):
        low, high = first_and_last(coords, d)
        packed = jnp.where(lane == d, low, packed)
        packed = jnp.where(lane == 3 + d, high, packed)
        for t in range(LEAVES):
            packed = jnp.where(lane == 8 + 3 * t + d, coords[d, t], packed)
    place[...] = packed.astype(F32)
    places[1] = place[...]
    pl.semaphore_wait(barrier, len(peers))

    hot_a = []
    for n, d in enumerate(FAR_FIRST):
        to = (j + d) % ROW
        copy = remote(
            rows.at[:, lanes(to * 256, 256)], first.at[j], h_send.at[0, n], h_recv.at[0, n], row_peers[n]
        )
        copy.start()
        hot_a.append(copy)
    wide = []
    for n, o in enumerate(chips):
        kk = (me + 2 * o + N_DOM) // 4 - base
        slot = 2 * (SPAN - o) + core
        copy = remote(stage.at[kk], window.at[slot], w_send.at[0, n], w_recv.at[0, n], window_peers[n])
        copy.start()
        wide.append(copy)
    own = window.at[2 * SPAN + core]
    shared_out = [remote(own, own, w_send.at[1, 8], w_recv.at[1, 8], sibling)]
    shared_out[0].start()
    beside = [
        remote(place, places.at[0], e_send.at[2], e_recv.at[2], {"dom": around[2]}),
        remote(place, places.at[2], e_send.at[3], e_recv.at[3], {"dom": around[0]}),
    ]
    for copy in beside + loads[6:]:
        copy.start()

    arrived(hot_a)
    piece = choose([first[s] for s in range(ROW)], hot % ROW)
    passed[...] = piece
    second[y] = piece
    hot_b = send_all(passed, second.at[y], h_send, h_recv, 1, column_peers)
    gap = iota((BW, 640), 1) - iota((BW, 640), 0)
    for k in range(2, NEAR_B):
        block = near[0, k]
        slot = (block // 4 - chip + SPAN + N_DOM // 2) % (N_DOM // 2) * 2 + block // 2 % 2
        start = slot * 32 + block % 2 * BW
        part = jnp.where(gap == start, 1.0, 0.0)[:, : 32 * HELD]
        pick_rows[(k - 2) * BW : (k - 1) * BW, :] = part.astype(BF16)
    wide_lane = iota((1, LEAF), 1)
    start = jnp.zeros((1, LEAF), jnp.int32)
    for k in range(NEAR_B):
        block = near[0, k]
        chunk = 5 if k < 2 else (block // 8 - me // 4 + 18) % 16
        start = jnp.where(wide_lane // BW == k, chunk * CHUNK + block % 8 * BW, start)
    start = start + wide_lane % BW
    pick = jnp.where(iota((WIDE, LEAF), 0) == start, 1.0, 0.0)
    pick_columns[...] = pick.astype(BF16)

    for n, o in enumerate(chips):
        wide[n].wait_recv()
        piece = window.at[2 * (SPAN - o) + core]
        copy = remote(piece, piece, w_send.at[1, n], w_recv.at[1, n], sibling)
        copy.start()
        shared_out.append(copy)
    arrived(hot_b)
    piece = choose([second[s] for s in range(ROW)], hot // ROW)
    kept[...] = piece
    hot_rows[j] = piece
    hot_c = send_all(kept, hot_rows.at[j], h_send, h_recv, 2, row_peers)
    for copy in loads[4:]:
        copy.wait()
    arrived(shared_out)
    held = window[...].reshape(32 * HELD, WIDE)
    chosen[...] = jnp.dot(pick_rows[...], held, preferred_element_type=F32).astype(BF16)
    matrix = jnp.dot(chosen[...], pick_columns[...], preferred_element_type=F32)
    local_matrix[0:32, :] = jnp.zeros((32, LEAF), BF16)
    local_matrix[32:, :] = matrix.astype(BF16)

    def window_density(t, carry):
        here = pl.ds(pl.multiple_of(t * LEAF, LEAF), LEAF)
        values = orbitals[here, :]
        product = jnp.dot(values, local_matrix[...], preferred_element_type=F32)
        product = product * values.astype(F32)
        folded[here, :] = (product[:, :128] + product[:, 128:256]) + (
            product[:, 256:384] + product[:, 384:]
        )
        return carry

    lax.fori_loop(0, LEAVES, window_density, 0)

    arrived(hot_c)
    parts = []
    for c in range(5):
        chunk = (me // 4 + 14 + c) % 16
        parts.append(hot_rows[chunk // 2, :, lanes(chunk % 2 * CHUNK, CHUNK)])
    options = [hot_rows[a, :, b * CHUNK : (b + 1) * CHUNK] for a in range(ROW) for b in range(2)]
    parts.append(choose(options, hot // 4))
    matrix = jnp.dot(
        jnp.concatenate(parts, axis=1), pick_columns[...], preferred_element_type=F32
    )
    matrix = jnp.concatenate([matrix, jnp.zeros((96, LEAF), F32)], axis=0).astype(BF16)

    total = jnp.zeros((1, R), F32)
    for t in range(LEAVES):
        here = slice(t * LEAF, (t + 1) * LEAF)
        values = orbitals[here, :]
        product = lax.dot_general(
            values, matrix, (((1,), (1,)), ((), ())), preferred_element_type=F32
        )
        product = product * values[:, :128].astype(F32) + folded[here, :]
        dense = jnp.sum(product.T, axis=0, keepdims=True)
        for i in range(4):
            rho[t * 4 + i : t * 4 + i + 1, :] = dense[:, i * 128 : (i + 1) * 128]
        leaf_moments = jnp.sum(basis[:, here] * dense, axis=1, keepdims=True)
        total = total + jnp.sum(transfer[t] * leaf_moments, axis=0, keepdims=True)
    mine = total
    edge = [
        remote(rho, halo.at[0], e_send.at[0], e_recv.at[0], {"dom": around[2]}),
        remote(rho, halo.at[1], e_send.at[1], e_recv.at[1], {"dom": around[0]}),
    ]
    upward = jnp.sum(dev_transfer[0] * to_column(mine), axis=0, keepdims=True)
    beyond = pltpu.roll(place[...], R, 1)
    mom_mine[0:1, :] = jnp.where(lane < R, jnp.concatenate([mine, mine], axis=1), beyond)
    mom_mine[1:2, :] = jnp.concatenate([upward, upward], axis=1)
    mom_row[j] = mom_mine[...]
    mom_a = send_all(mom_mine, mom_row.at[j], u_send, u_recv, 0, row_peers)
    for copy in edge:
        copy.start()
    rho_store = pltpu.make_async_copy(rho, rho_h, store_sem.at[0])
    rho_store.start()
    zero[...] = jnp.zeros_like(zero)
    zero_store = pltpu.make_async_copy(zero, zero_h, store_sem.at[2])
    zero_store.start()

    loads[3].wait()
    arrived(beside)
    for s in range(3):
        held = places[s]
        for t in range(LEAVES):
            for d in range(3):
                k = 8 + 3 * t + d
                spots[s * LEAVES + t, d : d + 1, :] = jnp.broadcast_to(held[:, k : k + 1], (1, 128))
    q = iota((64, 128), 0)
    p = iota((64, 128), 1) % 64
    gap_y = (p // 8 - q // 8).astype(F32)
    gap_z = (p % 8 - q % 8).astype(F32)
    step = (2 * iota((8, 128), 0) + iota((8, 128), 1) // 64 - 7).astype(F32)

    def build(t, carry):
        here = spots[LEAVES + t]
        for n in range(NEARL):
            w = near_leaves[n, t]
            shift = SIDE * (here - spots[w])
            x = step + shift[0:1, :]
            yy, zz = gap_y + shift[1:2, :], gap_z + shift[2:3, :]
            x, flat = x * x, yy * yy + zz * zz + 1.0
            for i in range(8):
                high, low = split(lax.rsqrt(flat + x[i : i + 1, :]))
                tables[t, 128 * n : 128 * n + 64, 128 * i : 128 * i + 128] = high
                tables[t, 128 * n + 64 : 128 * n + 128, 128 * i : 128 * i + 128] = low
        return carry

    lax.fori_loop(0, LEAVES // 2, build, 0)

    arrived(mom_a)
    sums, low, high = jnp.zeros((2, 128), F32), mom_row[0], mom_row[0]
    for b in range(ROW):
        value = mom_row[b]
        bundle[b] = value[0:1]
        sums, low, high = sums + value, jnp.minimum(low, value), jnp.maximum(high, value)
    bounds = jnp.where(lane < R + 3, low[0:1], high[0:1])
    bundle[ROW] = jnp.where(lane < R, sums[1:2], bounds)
    mom_all[y] = bundle[...]
    mom_b = send_all(bundle, mom_all.at[y], u_send, u_recv, 1, column_peers)

    arrived(edge)
    inside = [jnp.where(me > 0, 1.0, 0.0), 1.0, jnp.where(me < N_DOM - 1, 1.0, 0.0)]
    for s, held in enumerate((halo[0], rho[...], halo[1])):
        held = held * inside[s]
        rho_rows[pl.ds(48 * s, 24, stride=2), :] = held[:, :64]
        rho_rows[pl.ds(48 * s + 1, 24, stride=2), :] = held[:, 64:]
    for w in range(3 * LEAVES):
        high, low = split(rho_rows[8 * w : 8 * w + 8, :])
        sources[w] = jnp.concatenate(
            [jnp.concatenate([high, high], axis=1), jnp.concatenate([low, low], axis=1)], axis=0
        )

    def one_near(t, carry):
        lhs = jnp.concatenate([sources[near_leaves[n, t]] for n in range(NEARL)], axis=1)
        both = jnp.dot(lhs, tables[t], preferred_element_type=F32)
        both = both[:8] + both[8:]
        value = jnp.zeros((1, LEAF), F32)
        for qx in range(SIDE):
            value = value + both[qx : qx + 1, (7 - qx) * 64 : (7 - qx) * 64 + LEAF]
        for i in range(4):
            out[pl.ds(4 * t + i, 1), :] = value[:, 128 * i : 128 * i + 128] * vol_weight
        return carry

    lax.fori_loop(0, LEAVES // 2, one_near, 0)
    lax.fori_loop(LEAVES // 2, LEAVES, build, 0)

    arrived(mom_b)
    sums, low, high = jnp.zeros((1, 128), F32), mom_all[0, ROW], mom_all[0, ROW]
    for a in range(ROW):
        value = mom_all[a, ROW]
        sums, low, high = sums + value, jnp.minimum(low, value), jnp.maximum(high, value)
    bounds = jnp.where(lane < R + 3, low, high)
    mom_total[...] = jnp.where(lane < R, sums, bounds)
    mom_groups[group] = mom_total[...]
    mom_c = send_all(mom_total, mom_groups.at[group], u_send, u_recv, 2, group_peers)

    far_rows[...] = jnp.zeros_like(far_rows)
    for a in range(ROW):
        for b in range(ROW):
            n = a * ROW + b
            far_rows[n : n + 1, :] = mom_all[a, b]
    mask = jnp.concatenate([dev_far[...], jnp.zeros((1, 128 - N_DOM), jnp.int32)], axis=1)
    flipped = far_rows[...].T
    weights, edges = flipped[:R] * mask.astype(F32), flipped[R : R + 8]
    own, other = [], []
    for d in range(3):
        low, high = SIDE * edges[d : d + 1], SIDE * edges[3 + d : 4 + d] + (SIDE - 1)
        own_low, own_high = first_and_last(coords, d)
        own_low = jnp.full((1, 128), SIDE * own_low).astype(F32)
        own_high = jnp.full((1, 128), SIDE * own_high + (SIDE - 1)).astype(F32)
        own.append((0.5 * (own_low + own_high), 0.5 * (own_high - own_low)))
        other.append((0.5 * (low + high), 0.5 * (high - low)))
    sub = iota((8, 128), 0)
    sites = [[c + h * x for x in CHEB_X] for c, h in own]
    xs = [other[0][0] + other[0][1] * x for x in CHEB_X]
    ys = [other[1][0] + other[1][1] * spread(2 * half + sub // 4, (8, 128)) for half in range(2)]
    zs = other[2][0] + other[2][1] * spread(sub % 4, (8, 128))
    dx = [[(s - x) * (s - x) for x in xs] for s in sites[0]]
    dy = [[(s - v) * (s - v) for v in ys] for s in sites[1]]
    dz = [(s - zs) * (s - zs) + 1.0 for s in sites[2]]
    for b in range(CHEB):
        for e in range(CHEB):
            rest = [v + dz[e] for v in dy[b]]
            for a in range(CHEB):
                running = jnp.zeros((8, 128), F32)
                for t in range(8):
                    value = lax.rsqrt(dx[a][t // 2] + rest[t % 2])
                    running = running + value * weights[8 * t : 8 * t + 8]
                r = a * 16 + b * 4 + e
                partial[8 * r : 8 * r + 8, :] = running
    summed = partial[pl.ds(0, R, stride=8), :]
    for k in range(1, 8):
        summed = summed + partial[pl.ds(k, R, stride=8), :]
    dev_local = jnp.sum(summed, axis=1, keepdims=True)
    node = iota((R, 128), 0)
    point = iota((1, 128), 1) % 64
    own_nodes, far_steps = [], []
    for d, scale in enumerate((16, 4, 1)):
        own_low, own_high = SIDE * bounds[:, R + d : R + d + 1], bounds[:, R + 3 + d : R + 4 + d]
        own_high = SIDE * own_high + (SIDE - 1)
        centre, half = 0.5 * (own_low + own_high), 0.5 * (own_high - own_low)
        own_nodes.append(centre + half * spread(node // scale % 4, (R, 128)))
        far_steps.append(spread(point // scale % 4, (1, 128)))

    lax.fori_loop(LEAVES // 2, LEAVES, one_near, 0)

    arrived(mom_c)
    left = lane < R
    summed = jnp.zeros((R, 128), F32)
    for i in range(N_GROUP // 2):
        one, two = mom_groups[2 * i], mom_groups[2 * i + 1]
        square = jnp.full((R, 128), 1.0, F32)
        for d in range(3):
            at, to = slice(R + d, R + d + 1), slice(R + 3 + d, R + 4 + d)
            low = SIDE * jnp.where(left, one[:, at], two[:, at])
            high = jnp.where(left, one[:, to], two[:, to])
            high = SIDE * high + (SIDE - 1)
            gap = own_nodes[d] - (0.5 * (low + high) + 0.5 * (high - low) * far_steps[d])
            square = square + gap * gap
        mask = jnp.where(left, group_far[0, 2 * i], group_far[0, 2 * i + 1]).astype(F32)
        weight = jnp.concatenate([one[:, :R], two[:, :R]], axis=1) * mask
        summed = summed + lax.rsqrt(square) * weight
    group_local = to_row(jnp.sum(summed, axis=1, keepdims=True))
    dev_total = dev_local + jnp.sum(dev_transfer[0] * group_local, axis=1, keepdims=True)
    dev_total = to_row(dev_total * vol_weight)
    for t in range(LEAVES):
        leaf_local = jnp.sum(transfer[t] * dev_total, axis=1, keepdims=True)
        far = jnp.sum(basis[:, t * LEAF : (t + 1) * LEAF] * leaf_local, axis=0, keepdims=True)
        for i in range(4):
            out[4 * t + i : 4 * t + i + 1, :] += far[:, 128 * i : 128 * i + 128]
    out_store = pltpu.make_async_copy(out, out_h, store_sem.at[1])
    out_store.start()
    for copy in hot_a + hot_b + hot_c + wide + shared_out + beside + mom_a + mom_b + mom_c + edge:
        copy.wait_send()
    rho_store.wait()
    zero_store.wait()
    out_store.wait()


def local(
    orbitals, density_rows, near_blocks, leaf_coords, near_leaves, leaf_basis, leaf_transfer,
    dev_transfer, dev_far, group_far,
):
    anywhere = pl.BlockSpec(memory_space=pl.ANY)
    rows = pltpu.VMEM((1, 128), F32)
    slab = pltpu.VMEM((4 * LEAVES, 128), F32)
    sems = pltpu.SemaphoreType.DMA
    density, hartree, zero = pl.pallas_call(
        kernel,
        out_shape=(jax.ShapeDtypeStruct((4 * LEAVES, 128), F32),) * 3,
        in_specs=[anywhere] * 10,
        out_specs=(anywhere,) * 3,
        scratch_shapes=[
            pltpu.SMEM((1, NEAR_B), jnp.int32),
            pltpu.SMEM((3, LEAVES), jnp.int32),
            pltpu.SMEM((NEARL, LEAVES), jnp.int32),
            pltpu.SMEM((1, N_GROUP), jnp.int32),
            pltpu.VMEM((1, N_DOM), jnp.int32),
            pltpu.VMEM((LEAVES * LEAF, LEAF), BF16),
            pltpu.VMEM((32, 16 * CHUNK), BF16),
            pltpu.VMEM((R, LEAVES * LEAF), F32),
            pltpu.VMEM((LEAVES, R, R), F32),
            pltpu.VMEM((1, R, R), F32),
            slab, slab, slab,
            pltpu.VMEM((5, 32, WIDE), BF16),
            pltpu.VMEM((HELD, 32, WIDE), BF16),
            pltpu.VMEM((ROW, 32, 256), BF16),
            pltpu.VMEM((32, 256), BF16),
            pltpu.VMEM((ROW, 32, 256), BF16),
            pltpu.VMEM((32, 256), BF16),
            pltpu.VMEM((ROW, 32, 256), BF16),
            rows,
            pltpu.VMEM((3, 1, 128), F32),
            pltpu.VMEM((2, 128), F32),
            pltpu.VMEM((ROW, 2, 128), F32),
            pltpu.VMEM((ROW + 1, 1, 128), F32),
            pltpu.VMEM((ROW, ROW + 1, 1, 128), F32),
            rows,
            pltpu.VMEM((N_GROUP, 1, 128), F32),
            pltpu.VMEM((2, 4 * LEAVES, 128), F32),
            pltpu.VMEM((LEAF - 32, 32 * HELD), BF16),
            pltpu.VMEM((WIDE, LEAF), BF16),
            pltpu.VMEM((LEAF - 32, WIDE), BF16),
            pltpu.VMEM((LEAF, LEAF), BF16),
            pltpu.VMEM((LEAVES * LEAF, 128), F32),
            pltpu.VMEM((24 * LEAVES, 64), F32),
            pltpu.VMEM((3 * LEAVES, 16, 128), BF16),
            pltpu.VMEM((3 * LEAVES, 8, 128), F32),
            pltpu.VMEM((LEAVES, 128 * NEARL, 1024), BF16),
            pltpu.VMEM((128, 128), F32),
            pltpu.VMEM((8 * R, 128), F32),
            sems((10,)), sems((3,)),
            sems((2, 9)), sems((2, 9)),
            sems((3, ROW - 1)), sems((3, ROW - 1)),
            sems((3, ROW - 1)), sems((3, ROW - 1)),
            sems((4,)), sems((4,)),
        ],
        compiler_params=pltpu.CompilerParams(
            collective_id=0, has_side_effects=True, vmem_limit_bytes=60 << 20
        ),
    )(
        near_blocks, leaf_coords, near_leaves.T, group_far, dev_far, orbitals, density_rows,
        leaf_basis, leaf_transfer, dev_transfer,
    )
    return ((density + zero).reshape(-1), (hartree + zero).reshape(-1))


def solution(mesh):
    in_specs = (
        P(("group", "dom"), None),
        P(("group", "dom"), None),
        P(("group", "dom"), None),
        P(None, ("group", "dom")),
        P(("group", "dom"), None),
        P(None, ("group", "dom")),
        P(("group", "dom"), None, None),
        P(("group", "dom"), None, None),
        P(("group", "dom"), None),
        P("group", None),
    )
    out_specs = (P(("group", "dom")), P(("group", "dom")))
    return jax.shard_map(local, mesh=mesh, in_specs=in_specs, out_specs=out_specs, check_vma=False)
```
